32 devices in a mesh: group: 2 (over y), ctx: 4 (over z), head: 2 (over x), req: 2 (over core).
Axes of the slice: x: 2, y: 2, z: 4, core: 2. Of those that a mesh axis runs over, the one named last changes fastest.
Arguments:
- kda_query: bfloat16 [4, 768, 4096], P(('group', 'req'), 'ctx', 'head'), parts along dimension 0, may hold values from -6 to 6
- kda_key: bfloat16 [4, 768, 4096], P(('group', 'req'), 'ctx', 'head'), parts along dimension 0, may hold values from -6 to 6
- kda_value: bfloat16 [4, 768, 4096], P(('group', 'req'), 'ctx', 'head'), parts along dimension 0, may hold values from -6 to 6
- log_decay: bfloat16 [4, 768, 4096], P(('group', 'req'), 'ctx', 'head'), parts along dimension 0, may hold values from -1 to 0
- write_strength: float32 [4, 32, 768], P(('group', 'req'), 'head', 'ctx'), parts along dimension 0, may hold values from 0.1 to 0.95
- mla_query: bfloat16 [4, 768, 18432], P(('group', 'req'), 'ctx', 'head'), parts along dimension 0, may hold values from -18 to 18
- latents: bfloat16 [4, 768, 576], P(('group', 'req'), 'ctx'), parts along dimension 0, may hold values from -8 to 8
- value_up: bfloat16 [32, 512, 128], P('head'), may hold values from -0.25 to 0.25
- out_proj: bfloat16 [4096, 2304], P('head'), may hold values from -0.09375 to 0.09375
- doc_lengths: int32 [4, 8], P(('group', 'req')), parts along dimension 0, may hold values from 1 to 288, 768 in all within a row
Outputs:
- kda_out: bfloat16 [4, 768, 4096], P(('group', 'req'), 'ctx', 'head'), parts along dimension 0
- mixed: bfloat16 [4, 768, 2304], P(('group', 'req'), ('ctx', 'head')), parts along dimension 0
The draws below stay inside these ranges and needn't reach their ends.
There are 2 independent parts, one for each index of `group`. The reference program is written for one: setup_inputs(seed, part) draws one part's arguments, and reference() takes and returns one part's arrays. A program takes and returns all parts, laid end to end along the dimension named above; an argument that names none is the same for every part. Nothing has to cross between parts.
Inputs may be any that keep to these rules, and one draw needn't show every extreme that they name: `doc_lengths`: each row's lengths sum to 768, and each row's longest prompt has exactly 288 positions.
All inputs are finite; a program needn't handle non-finite values.
Results may differ from the reference program's by a relative error of at most 0.009.
Values may be sent and summed in bfloat16 or wider, within the bound.
A program may use at most 128 MiB of HBM per device.

```python
import math
import jax
import jax.numpy as jnp
import numpy as np
from jax import lax

HEAD_COUNT = 32
STATE = 128
LATENT = 512
ROPE = 64
NOPE = 128
VHEAD = 128
MODEL = 2304
TOK_DEV = 192
DOCS = 8
PACKED_ROWS = 2
ROW_LENGTH = 768


def draw_log_decay(key, part):
    base = jax.random.fold_in(key, 3)
    piece_keys = jax.random.split(base, 8)
    fast_share = 0.5
    is_fast = jax.random.bernoulli(piece_keys[0], fast_share, (HEAD_COUNT,))
    fast_rate = jnp.exp(jax.random.uniform(piece_keys[1], (HEAD_COUNT,), jnp.float32, math.log(1.0 / 50.0), math.log(1.0 / 30.0)))
    slow_rate = jnp.exp(jax.random.uniform(piece_keys[2], (HEAD_COUNT,), jnp.float32, math.log(0.02), math.log(0.2))) / ROW_LENGTH
    head_rate = jnp.where(is_fast, fast_rate, slow_rate)
    channel_factor = jnp.exp(jax.random.uniform(piece_keys[3], (HEAD_COUNT, STATE), jnp.float32, math.log(0.6), math.log(1.6)))
    blocks_total = ROW_LENGTH // TOK_DEV
    block_multiplier = jnp.exp(jax.random.uniform(piece_keys[4], (PACKED_ROWS, blocks_total, 1, 1), jnp.float32, math.log(0.6), math.log(1.6)))
    block_multiplier = jnp.repeat(block_multiplier, TOK_DEV, axis=1)
    small_noise = jax.random.uniform(piece_keys[5], (PACKED_ROWS, ROW_LENGTH, HEAD_COUNT, STATE), jnp.float32, 0.5, 1.5)
    surge_positions = jax.random.randint(piece_keys[6], (PACKED_ROWS, 3), 0, ROW_LENGTH)
    position_list = jnp.arange(ROW_LENGTH, dtype=jnp.int32)
    surging_flag = jnp.any(surge_positions[:, None, :] == position_list[None, :, None], axis=2).astype(jnp.float32)
    surge_depth = jax.random.uniform(piece_keys[7], (PACKED_ROWS, ROW_LENGTH, HEAD_COUNT, 1), jnp.float32, 0.223, 0.693)
    decay_rates = (head_rate[:, None] * channel_factor)[None, None]
    layer_result = -(decay_rates * block_multiplier * small_noise) - surging_flag[:, :, None, None] * surge_depth
    return layer_result.reshape(PACKED_ROWS, ROW_LENGTH, HEAD_COUNT * STATE).astype(jnp.bfloat16)


def mla_pair(key):
    width = LATENT + ROPE
    key_latent = jax.random.fold_in(key, 21)
    key_query = jax.random.fold_in(key, 22)
    latent_rows = jax.random.truncated_normal(key_latent, -4.0, 4.0, (PACKED_ROWS, ROW_LENGTH, width), jnp.float32)
    query_rows = jax.random.truncated_normal(key_query, -4.0, 4.0, (PACKED_ROWS, ROW_LENGTH, HEAD_COUNT, width), jnp.float32)
    return (query_rows.reshape(PACKED_ROWS, ROW_LENGTH, HEAD_COUNT * width), latent_rows)


def draw_mla_query(key, part):
    return mla_pair(key)[0].astype(jnp.bfloat16)


def draw_latents(key, part):
    return mla_pair(key)[1].astype(jnp.bfloat16)


def shard_levels(own_key, dims, cuts, smallest, high):
    factor_of, own = 1.0, jax.random.fold_in(own_key, 6)
    for dim, shards_of in cuts:
        heights = jnp.exp(jax.random.uniform(jax.random.fold_in(own, dim), (shards_of,), jnp.float32, smallest / len(cuts), high / len(cuts)))
        factor_of = factor_of * jnp.repeat(heights, dims[dim] // shards_of).reshape([-1 if axis == dim else 1 for axis in range(len(dims))])
    return factor_of


def profile(amount, total, most, slope):
    loads = [(1 << 20) // math.isqrt(standing ** slope) + 1 for standing in range(2, amount + 1)]
    rest, counts = total - most - (amount - 1), [1] * (amount - 1)
    while rest > 0:
        free = [i for i in range(amount - 1) if counts[i] < most]
        whole, budget = sum([loads[i] for i in free]), rest
        for i in free:
            more = min(most - counts[i], max(1, budget * loads[i] // whole), rest)
            counts[i] = counts[i] + more
            rest = rest - more
    return np.array([most] + counts)


def ragged(stream_key, number_of, total, bound, slope):
    if number_of == 2:
        one = jax.random.randint(stream_key, (), max(1, total - bound), min(bound, total - 1) + 1)
        return jnp.stack([one, total - one])
    sizes = jnp.asarray(profile(number_of, total, bound, slope), jnp.int32)
    twos = (number_of - 1) // 2
    donor, taker = sizes[1:1 + 2 * twos:2], sizes[2:2 + 2 * twos:2]
    room = jnp.minimum(donor - 1, bound - taker)
    moved = jax.random.randint(jax.random.fold_in(stream_key, 1), (twos,), 0, 1 << 20) % (room + 1)
    sizes = sizes.at[1:1 + 2 * twos:2].set(donor - moved).at[2:2 + 2 * twos:2].set(taker + moved)
    return sizes[jax.random.permutation(jax.random.fold_in(stream_key, 2), number_of)]


def noise(own_key, extent, scale, bound, pieces=(), kind=jnp.bfloat16):
    values = jax.random.normal(own_key, extent, jnp.float32) * scale
    if len(pieces) > 0:
        values = shard_levels(own_key, extent, pieces, -0.22, 0.18) * values
    return jnp.clip(values, min=-bound, max=bound).astype(kind)


def setup_inputs(seed: int = 0, part: int = 0) -> dict:
    key_of = jax.random.split(jax.random.key(seed), 11)
    own_keys = jax.random.split(jax.random.fold_in(key_of[10], part), 11)
    return {
        "kda_query": noise(own_keys[0], (PACKED_ROWS, ROW_LENGTH, HEAD_COUNT * STATE), 1.0, 6.0, ((0, 2), (1, 4), (2, 2))),
        "kda_key": noise(own_keys[1], (PACKED_ROWS, ROW_LENGTH, HEAD_COUNT * STATE), 1.0, 6.0, ((0, 2), (1, 4), (2, 2))),
        "kda_value": noise(own_keys[2], (PACKED_ROWS, ROW_LENGTH, HEAD_COUNT * STATE), 1.0, 6.0, ((0, 2), (1, 4), (2, 2))),
        "log_decay": draw_log_decay(jax.random.fold_in(jax.random.fold_in(key_of[10], part), 71), part),
        "write_strength": jnp.clip(0.1 + 0.84999999 * jax.random.uniform(own_keys[4], (PACKED_ROWS, HEAD_COUNT, ROW_LENGTH), jnp.float32) ** shard_levels(own_keys[4], (PACKED_ROWS, HEAD_COUNT, ROW_LENGTH), ((0, 2), (1, 2), (2, 4)), -0.2, 0.2), 0.1, 0.95),
        "mla_query": draw_mla_query(jax.random.fold_in(jax.random.fold_in(key_of[10], part), 71), part),
        "latents": draw_latents(jax.random.fold_in(jax.random.fold_in(key_of[10], part), 71), part),
        "value_up": noise(key_of[7], (HEAD_COUNT, LATENT, VHEAD), LATENT ** -0.5, 0.25, ((0, 2),)),
        "out_proj": noise(key_of[8], (HEAD_COUNT * VHEAD, MODEL), (HEAD_COUNT * VHEAD) ** -0.5, 0.09375, ((0, 2),)),
        "doc_lengths": jax.vmap(lambda own: ragged(own, DOCS, ROW_LENGTH, 3 * ROW_LENGTH // DOCS, 2))(jax.random.split(own_keys[9], PACKED_ROWS)).reshape((PACKED_ROWS, DOCS)).astype(jnp.int32),
    }


top_value = lax.Precision.HIGHEST
masked_score = -1e+30

def unit_length(values):
    values = values.astype(jnp.float32)
    return values * lax.rsqrt(lax.optimization_barrier(jnp.sum(values * values, axis=-1, keepdims=True)) + 1e-06)

def reference(kda_query, kda_key, kda_value, log_decay, write_strength, mla_query, latents, value_up, out_proj, doc_lengths):
    positions = jnp.arange(ROW_LENGTH, dtype=jnp.int32)
    doc_ends = jnp.cumsum(doc_lengths, axis=1).astype(jnp.int32)
    doc_starts = (doc_ends - doc_lengths).astype(jnp.int32)
    doc_ids = lax.optimization_barrier(jnp.sum((doc_ends[:, None, :] <= positions[None, :, None]).astype(jnp.int32), axis=2)).astype(jnp.int32)
    opening = jnp.any(doc_starts[:, None, :] == positions[None, :, None], axis=2)
    head_shape = (PACKED_ROWS, ROW_LENGTH, HEAD_COUNT, STATE)
    query_rows = unit_length(kda_query.reshape(head_shape))
    key_rows = unit_length(kda_key.reshape(head_shape))
    value_rows = kda_value.reshape(head_shape).astype(jnp.float32)
    gate_rows = jnp.exp(log_decay.reshape(head_shape).astype(jnp.float32))
    strength = jnp.transpose(write_strength, (0, 2, 1)).astype(jnp.float32)

    def advance(state_now, inputs):
        query_t, key_t, value_t, gate_t, beta_t, open_t = inputs
        state_now = jnp.where(open_t[:, None, None, None], jnp.zeros_like(state_now), gate_t[..., None] * state_now)
        recalled = jnp.einsum('shk,shkv->shv', key_t, state_now, precision=top_value)
        state_now = state_now + beta_t[..., None, None] * key_t[..., None] * (value_t - recalled)[..., None, :]
        return (state_now, jnp.einsum('shk,shkv->shv', query_t, state_now, precision=top_value))
    stepwise = tuple((jnp.moveaxis(member, 1, 0) for member in (query_rows, key_rows, value_rows, gate_rows, strength, opening)))
    start_state = jnp.zeros((PACKED_ROWS, HEAD_COUNT, STATE, STATE), jnp.float32)
    _, outputs = lax.scan(advance, start_state, stepwise)
    kda_out = jnp.moveaxis(outputs, 0, 1).reshape(PACKED_ROWS, ROW_LENGTH, HEAD_COUNT * STATE).astype(jnp.bfloat16)
    width = LATENT + ROPE
    score_scale = 1.0 / math.sqrt(NOPE + ROPE)
    causal = positions[None, :, None] >= positions[None, None, :]
    allowed = causal & (doc_ids[:, :, None] == doc_ids[:, None, :])
    latent_rows = latents.astype(jnp.float32)
    query_heads = jnp.moveaxis(mla_query.reshape(PACKED_ROWS, ROW_LENGTH, HEAD_COUNT, width), 2, 0)

    def one_head(query_head):
        scores = jnp.einsum('sik,sjk->sij', query_head.astype(jnp.float32), latent_rows) * score_scale
        row_peak = lax.optimization_barrier(jnp.max(jnp.where(allowed, scores, masked_score), axis=2, keepdims=True))
        exponent = jnp.where(allowed, jnp.exp(scores - row_peak), jnp.zeros_like(scores))
        row_total = lax.optimization_barrier(jnp.sum(exponent, axis=2, keepdims=True))
        weights = lax.optimization_barrier(exponent.astype(jnp.bfloat16)).astype(jnp.float32)
        mixed_lat = jnp.einsum('sij,sjl->sil', weights, latent_rows[:, :, :LATENT]) / row_total
        return mixed_lat.astype(jnp.bfloat16)
    context = lax.map(one_head, query_heads)
    head_out = jnp.einsum('hsil,hlv->sihv', context.astype(jnp.float32), value_up.astype(jnp.float32)).astype(jnp.bfloat16)
    head_out = head_out.reshape(PACKED_ROWS * ROW_LENGTH, HEAD_COUNT * VHEAD)
    mixed = jnp.dot(head_out, out_proj, preferred_element_type=jnp.float32).astype(jnp.bfloat16)
    return (kda_out, mixed.reshape(PACKED_ROWS, ROW_LENGTH, MODEL))
```

```python
import functools
import math

import jax
import jax.numpy as jnp
from jax import lax
from jax.experimental import pallas as pl
from jax.experimental.pallas import tpu as pltpu
from jax.sharding import PartitionSpec as P

ROPE = 64
NOPE = 128
MESH = pl.DeviceIdType.MESH
CHUNK = 256

masked_score = -1e30
ROWS = (((1,), (0,)), ((), ()))
TRANS = (((1,), (1,)), ((), ()))
OVER = (((0,), (0,)), ((), ()))


def in_place(value):
    return pltpu.with_memory_space_constraint(value, pltpu.HBM)


def dot_once(left, right, dims):
    return lax.dot_general(
        left.astype(jnp.bfloat16),
        right.astype(jnp.bfloat16),
        dims,
        preferred_element_type=jnp.float32,
    )


def pick(index, values):
    chosen = jnp.int32(values[0])
    for place, value in enumerate(values):
        if place > 0 and value != values[0]:
            chosen = jnp.where(index == place, jnp.int32(value), chosen)
    return chosen


def iota2(shape, axis):
    return lax.broadcasted_iota(jnp.int32, shape, axis)


def delta_setup(lengths_ref, strength_ref, rel_top, rel_bot, carried_ref, tail_ref, beta_ref, first, per_group):
    tokens, state_dim = carried_ref.shape
    top = rel_top.shape[0]
    wide = rel_bot.shape[1]
    bot = tokens - top
    pos_col = first + iota2((tokens, 1), 0)
    pos_row = first + iota2((1, wide), 1)
    doc_col, doc_row = jnp.zeros_like(pos_col), jnp.zeros_like(pos_row)
    prev_doc, last_doc, end = jnp.int32(0), jnp.int32(0), jnp.int32(0)
    for d in range(lengths_ref.shape[1]):
        end = end + lengths_ref[0, d]
        doc_col = doc_col + jnp.where(pos_col >= end, 1, 0)
        doc_row = doc_row + jnp.where(pos_row >= end, 1, 0)
        prev_doc = prev_doc + jnp.where(first - 1 >= end, 1, 0)
        last_doc = last_doc + jnp.where(first + tokens - 1 >= end, 1, 0)
    rel_top[...] = jnp.where(
        doc_col[:top] == doc_row[:, :top], iota2((top, top), 0) - iota2((top, top), 1), -1
    )
    rel_bot[...] = jnp.where(
        (doc_col[top:] == doc_row) & (iota2((bot, wide), 1) < tokens),
        iota2((bot, wide), 0) + top - iota2((bot, wide), 1),
        -1,
    )
    ones = jnp.ones((1, state_dim), jnp.float32)
    carried_ref[...] = jnp.where(doc_col == prev_doc, 1.0, 0.0) * ones
    tail_ref[...] = jnp.where(doc_col == last_doc, 1.0, 0.0) * ones
    heads = strength_ref.shape[0]
    padded = jnp.concatenate(
        [strength_ref[...], jnp.zeros((heads, wide - tokens), jnp.float32)], axis=1
    )
    padded = jnp.concatenate([padded, jnp.zeros((128 - heads, wide), jnp.float32)], axis=0)
    turned = jnp.transpose(padded)[:tokens]
    for g in range(heads // per_group):
        beta_ref[g] = turned if g == 0 else pltpu.roll(turned, 128 - g * per_group, 1)


def packed_inverse(pack):
    lane = iota2((1, 128), 1)
    piece = pack[0:16]
    for b in range(1, 4):
        piece = jnp.where((lane % 64) // 16 == b, pack[16 * b : 16 * b + 16], piece)
    row16, col16 = iota2((16, 128), 0), iota2((16, 128), 1) % 16
    inv = jnp.where((row16 // 2 == col16 // 2) & (row16 > col16), -piece, 0.0)
    yield
    for width, size in ((2, 16), (4, 16), (8, 16), (16, 32), (32, 64)):
        if size == 32:
            piece = jnp.where((lane % 64) // 32 == 0, pack[0:32], pack[32:64])
        elif size == 64:
            piece = pack
        if width == size // 2 and size > 16:
            inv = jnp.concatenate(
                [
                    jnp.where(lane % size < width, inv, 0.0),
                    jnp.where(lane % size >= width, inv, 0.0),
                ],
                axis=0,
            )
        row, col = iota2((size, 128), 0), iota2((size, 128), 1) % size
        corner = (row // (2 * width) == col // (2 * width)) & (row // width > col // width)
        part = jnp.where(corner, piece, 0.0)
        left = part + dot_once(inv, spread(part, size), ROWS)
        yield
        inv = inv - (left + dot_once(left, spread(inv, size), ROWS))
        yield
    yield inv


def spread(cells, size):
    copies = 128 // size
    own = iota2((128, 128), 0) // size == iota2((128, 128), 1) // size
    return jnp.where(own, jnp.concatenate([cells] * copies, axis=0), 0.0).astype(jnp.bfloat16)


def together(makers):
    done = []
    while True:
        step = [next(m) for m in makers]
        if step[0] is not None:
            return step


def delta_group(
    g, per_group, query_ref, key_ref, value_ref, decay_ref, beta_ref, rel_top, rel_bot,
    carried_ref, tail_ref, readout_ref, local_ref, transition_ref, offset_ref,
):
    tokens, state_dim = carried_ref.shape
    top = rel_top.shape[0]
    half = top // 2
    heads = range(per_group)
    inclusive = jnp.where(
        iota2((tokens, tokens), 0) >= iota2((tokens, tokens), 1), 1.0, 0.0
    ).astype(jnp.bfloat16)
    lane = iota2((1, 128), 1)
    at = [
        pl.ds(pl.multiple_of((g * per_group + h) * state_dim, state_dim), state_dim) for h in heads
    ]
    summed = []
    for h in range(0, per_group, 2):
        both = pl.ds(
            pl.multiple_of((g * per_group + h) * state_dim, 2 * state_dim), 2 * state_dim
        )
        pair = jnp.dot(inclusive, decay_ref[:, both], preferred_element_type=jnp.float32)
        summed += [pair[:, :state_dim], pair[:, state_dim:]]
    lower_top, lower_bot, attend_top, attend_bot = [], [], [], []
    right_keys, read_query, key_decay, kept, rights = [], [], [], [], []
    for h in heads:
        s = summed[h]
        query = query_ref[:, at[h]].astype(jnp.float32)
        key = key_ref[:, at[h]].astype(jnp.float32)
        beta = beta_ref[g, :, h : h + 1]
        query = query * lax.rsqrt(jnp.sum(query * query, axis=1, keepdims=True) + 1e-06)
        key = key * lax.rsqrt(jnp.sum(key * key, axis=1, keepdims=True) + 1e-06)
        written = key * beta
        mid, start, last = s[half - 1 : half], s[top - 1 : top], s[tokens - 1 : tokens]
        fall_top, fall_bot = jnp.exp(s[:top] - mid), jnp.exp(s[top:] - start)
        lift_top, lift_bot = jnp.exp(mid - s[:top]), jnp.exp(start - s[top:])
        to_mid, to_start, mid_start = jnp.exp(mid), jnp.exp(start), jnp.exp(start - mid)
        key_top, key_bot = written[:top] * fall_top, written[top:] * fall_bot
        query_top, query_bot = query[:top] * fall_top, query[top:] * fall_bot
        raised_top = key[:top] * lift_top
        raised_all = jnp.concatenate([raised_top * mid_start, key[top:] * lift_bot], axis=0)
        both_top = dot_once(
            jnp.concatenate([key_top, query_top], axis=0), raised_top, TRANS
        )
        both_bot = dot_once(
            jnp.concatenate([key_bot, query_bot], axis=0),
            jnp.concatenate([raised_all, jnp.zeros((half, state_dim), jnp.float32)], axis=0),
            TRANS,
        )
        lower_top.append(jnp.where(rel_top[...] > 0, both_top[:top], 0.0))
        attend_top.append(jnp.where(rel_top[...] >= 0, both_top[top:], 0.0).astype(jnp.bfloat16))
        lower_bot.append(jnp.where(rel_bot[...] > 0, both_bot[:half], 0.0))
        attend_bot.append(
            jnp.where(rel_bot[...] >= 0, both_bot[half:], 0.0).astype(jnp.bfloat16)
        )
        carried = carried_ref[...]
        grown = jnp.concatenate([key_top * to_mid, key_bot * to_start], axis=0) * carried
        read_query.append(
            jnp.concatenate([query_top * to_mid, query_bot * to_start], axis=0) * carried
        )
        key_decay.append((raised_all * jnp.exp(last - start) * tail_ref[...]).astype(jnp.bfloat16))
        kept.append(jnp.exp(last) * carried[tokens - 1 : tokens])
        rights.append(
            jnp.concatenate([grown, value_ref[:, at[h]].astype(jnp.float32) * beta], axis=1)
        )
    makers = [
        packed_inverse(jnp.where(lane < half, lower_top[h][:half], lower_top[h][half:]))
        for h in heads
    ]
    makers += [
        packed_inverse(
            jnp.where(
                lane < half,
                lower_bot[h][:, top:],
                pltpu.roll(lower_bot[h + 1][:, top:], half, 1),
            )
        )
        for h in range(0, per_group, 2)
    ]
    inverses = together(makers)
    firsts, seconds, tops, wholes = [], [], [], []
    for h in heads:
        right = rights[h]
        inv = jnp.where(lane < half, inverses[h], 0.0)
        firsts.append(right[:half] + dot_once(inv, right[:top], ROWS))
    for h in heads:
        across = jnp.where(lane < half, lower_top[h][half:], 0.0)
        seconds.append(
            rights[h][half:top]
            - dot_once(across, jnp.concatenate([firsts[h]] * 2, axis=0), ROWS)
        )
    for h in heads:
        inv = jnp.where(lane >= half, inverses[h], 0.0)
        tops.append(
            jnp.concatenate(
                [
                    firsts[h],
                    seconds[h] + dot_once(inv, jnp.concatenate([seconds[h]] * 2, axis=0), ROWS),
                ],
                axis=0,
            ).astype(jnp.bfloat16)
        )
    thirds = [
        rights[h][top:] - dot_once(lower_bot[h][:, :top], tops[h], ROWS) for h in heads
    ]
    for h in heads:
        inv = inverses[per_group + h // 2]
        inv = jnp.where(lane < half, inv, 0.0) if h % 2 == 0 else jnp.where(lane >= half, inv, 0.0)
        third = thirds[h] + dot_once(inv, jnp.concatenate([thirds[h]] * 2, axis=0), ROWS)
        wholes.append(jnp.concatenate([tops[h], third.astype(jnp.bfloat16)], axis=0))
    eye = iota2((state_dim, state_dim), 0) == iota2((state_dim, state_dim), 1)
    for h in heads:
        moved = dot_once(key_decay[h], wholes[h], OVER)
        head = g * per_group + h
        transition_ref[head] = (
            jnp.where(eye, kept[h], 0.0) - moved[:, :state_dim]
        ).astype(transition_ref.dtype)
        offset_ref[head] = moved[:, state_dim:]
    for h in heads:
        read = dot_once(attend_top[h], tops[h], ROWS)
        readout_ref[:top, at[h]] = (read_query[h][:top] - read[:, :state_dim]).astype(
            readout_ref.dtype
        )
        local_ref[:top, at[h]] = read[:, state_dim:]
        read = dot_once(attend_bot[h][:, :tokens], wholes[h], ROWS)
        readout_ref[top:, at[h]] = (read_query[h][top:] - read[:, :state_dim]).astype(
            readout_ref.dtype
        )
        local_ref[top:, at[h]] = read[:, state_dim:]


def attend_step(
    half, step, group, query_ref, even_ref, odd_ref, bias_ref, up_ref, out_ref,
    *, width, first_key, key_count, score_scale,
):
    rows = out_ref.shape[0]
    wide = even_ref.shape[1]
    lat_dim, vhead = up_ref.shape[1:]
    pairs = group // 2
    keys = pl.ds(pl.multiple_of(half * rows + first_key, math.gcd(rows, first_key)), key_count)
    own = pl.ds(pl.multiple_of(half * rows, rows), rows)
    bias = bias_ref[half]
    contexts = []
    for key_ref, skip in ((even_ref, 0), (odd_ref, 2 * width - wide)):
        stacked = []
        for p in range(pairs):
            begin = (step * group + 2 * p) * width + skip
            stacked.append(query_ref[own, pl.ds(pl.multiple_of(begin, 128), wide)])
        query = jnp.concatenate(stacked, axis=0) if pairs > 1 else stacked[0]
        scores = lax.dot_general(
            query, key_ref[keys, :], TRANS, preferred_element_type=jnp.float32
        )
        scores = scores.reshape(pairs, rows, key_count) * score_scale + bias[None]
        exponent = jnp.exp(scores - jnp.max(scores, axis=2, keepdims=True))
        exponent = exponent.reshape(pairs * rows, key_count)
        row_total = jnp.sum(exponent, axis=1, keepdims=True)
        weighted = jnp.dot(
            exponent.astype(jnp.bfloat16),
            even_ref[keys, :lat_dim],
            preferred_element_type=jnp.float32,
        )
        contexts.append((weighted / row_total).astype(jnp.bfloat16))
    for p in range(pairs):
        for parity in range(2):
            head = step * group + 2 * p + parity
            out_ref[:, pl.ds(pl.multiple_of(head * vhead, vhead), vhead)] = jnp.dot(
                contexts[parity][p * rows : (p + 1) * rows],
                up_ref[head],
                preferred_element_type=jnp.float32,
            ).astype(jnp.bfloat16)


def layers(
    lengths_ref, kq_hbm, kk_hbm, kv_hbm, kg_hbm, strength_hbm, mq_hbm, lat_hbm, up_hbm, proj_hbm,
    kda_stage, mixed_stage,
    kq, kk, kv, kg, strength, mq, window, even, odd, up, proj,
    rel_top, rel_bot, carried, tail, beta, readout, local_part, transition, offset,
    state_out, state_in, bias, head_out, far_send, far_recv,
    kda_sem, load_sem, proj_sem, lat_send, lat_recv, pass_send, pass_recv,
    state_send, state_recv, far_ssem, far_rsem,
    *, hops, need, width, per_group, per_step, per_pass, first_key, key_count, score_scale, exchange,
):
    tokens, lanes = kq.shape
    heads = strength.shape[0]
    state_dim = lanes // heads
    groups = heads // per_group
    steps = heads // per_step
    passes = heads // per_pass
    rows = tokens // 2
    ctx_count = lax.axis_size("ctx")
    place = lax.axis_index("ctx")
    mine = lax.axis_index("head")
    model = proj.shape[1]
    pieces = model // CHUNK
    first = place * tokens

    def up_by(by):
        return {"ctx": place + by}

    partner = {"head": 1 - mine}

    def load(source, target, sem):
        copy = pltpu.make_async_copy(source, target, sem)
        copy.start()
        return copy

    strength_copy = load(strength_hbm.at[0], strength, load_sem.at[0])
    kda_copies = []
    for g in range(groups):
        part = pl.ds(g * per_group * state_dim, per_group * state_dim)
        kda_copies.append(
            [
                load(source.at[0, :, part], target.at[:, part], kda_sem.at[g, n])
                for n, (source, target) in enumerate(
                    ((kg_hbm, kg), (kq_hbm, kq), (kk_hbm, kk), (kv_hbm, kv))
                )
            ]
        )
    lat_copy = load(lat_hbm.at[0], window.at[pl.ds(hops * tokens, tokens)], load_sem.at[1])

    barrier = pltpu.get_barrier_semaphore()
    for by in range(1, hops + 1):
        for sign in (1, -1):
            there = place + sign * by

            @pl.when((there >= 0) & (there < ctx_count))
            def _():
                pl.semaphore_signal(
                    barrier, inc=1, device_id={"ctx": there}, device_id_type=MESH
                )

    peers = jnp.int32(0)
    for by in range(1, hops + 1):
        for sign in (1, -1):
            there = place + sign * by
            peers = peers + jnp.where((there >= 0) & (there < ctx_count), 1, 0)
    if exchange:
        pl.semaphore_signal(barrier, inc=1, device_id=partner, device_id_type=MESH)
        peers = peers + 1
    pl.semaphore_wait(barrier, peers)

    def lat_rows(by, which):
        count = need[by - 1] // 2 if exchange else need[by - 1]
        begin = tokens - need[by - 1]
        if exchange:
            begin = pl.multiple_of(begin + which * count, 16)
        return begin, count

    def lat_copy_to(by):
        begin, count = lat_rows(by, mine)
        return pltpu.make_async_remote_copy(
            src_ref=lat_hbm.at[0, pl.ds(begin, count)],
            dst_ref=window.at[pl.ds(begin + (hops - by) * tokens, count)],
            send_sem=lat_send.at[by - 1],
            recv_sem=lat_recv.at[by - 1],
            device_id=up_by(by),
            device_id_type=MESH,
        )

    def lat_pass(by):
        begin, count = lat_rows(by, mine)
        region = window.at[pl.ds(begin + (hops - by) * tokens, count)]
        return pltpu.make_async_remote_copy(
            src_ref=region,
            dst_ref=region,
            send_sem=pass_send.at[by - 1],
            recv_sem=pass_recv.at[by - 1],
            device_id=partner,
            device_id_type=MESH,
        )

    for by in range(1, hops + 1):

        @pl.when(place + by < ctx_count)
        def _():
            lat_copy_to(by).start()

        @pl.when(place < by)
        def _():
            window[(hops - by) * tokens : (hops - by + 1) * tokens] = jnp.zeros(
                (tokens, width), window.dtype
            )

    mq_copies = []
    for step in range(steps):
        part = pl.ds(step * per_step * width, per_step * width)
        mq_copies.append(load(mq_hbm.at[0, :, part], mq.at[:, part], load_sem.at[2 + step]))
    up_copy = load(up_hbm, up, load_sem.at[2 + steps])
    proj_copies = [
        load(
            proj_hbm.at[:, pl.ds(n * CHUNK, CHUNK)],
            proj.at[:, pl.ds(n * CHUNK, CHUNK)],
            proj_sem.at[n],
        )
        for n in range(pieces)
    ]

    def state_copy(c):
        part = pl.ds(c * per_pass, per_pass)
        return pltpu.make_async_remote_copy(
            src_ref=state_out.at[part],
            dst_ref=state_in.at[part],
            send_sem=state_send.at[c],
            recv_sem=state_recv.at[c],
            device_id=up_by(1),
            device_id_type=MESH,
        )

    def relay(c, _):
        @pl.when(place > 0)
        def _():
            state_copy(c).wait_recv()

        @pl.when(place == 0)
        def _():
            for n in range(per_pass):
                head = c * per_pass + n
                state_out[head] = offset[head].astype(state_out.dtype)

        @pl.when((place > 0) & (place + 1 < ctx_count))
        def _():
            for n in range(per_pass):
                head = c * per_pass + n
                state_out[head] = (
                    offset[head]
                    + jnp.dot(
                        transition[head], state_in[head], preferred_element_type=jnp.float32
                    )
                ).astype(state_out.dtype)

        @pl.when(place + 1 < ctx_count)
        def _():
            state_copy(c).start()

        return 0

    slots = groups + 2 * steps + 6
    passes_group = passes // groups
    slot_now = [0]

    def finished(slot, k):
        if slot >= slots - 1:
            return passes
        if k == 0:
            return min(passes, passes_group * (slot + 1))
        if k >= ctx_count - 1:
            return 0
        late = slot - groups - 2 * (k - 1)
        if slot < groups:
            return max(0, passes_group * (slot - k + 1) // 2) if k == 1 else 0
        return max(0, min(passes, passes_group * (groups - 1) + late + 1 - (k - 1)))

    def relay_slot():
        slot = slot_now[0]
        slot_now[0] += 1
        before = [0 if slot == 0 else finished(slot - 1, k) for k in range(ctx_count)]
        after = [finished(slot, k) for k in range(ctx_count)]
        after = [max(a, b) for a, b in zip(before, after)]
        if before != after:
            lax.fori_loop(pick(place, before), pick(place, after), relay, 0)

    @pl.when(place == 0)
    def _():
        state_in[...] = jnp.zeros_like(state_in)

    strength_copy.wait()
    delta_setup(
        lengths_ref, strength, rel_top, rel_bot, carried, tail, beta, first, per_group
    )
    for g in range(groups):
        for copy in kda_copies[g]:
            copy.wait()
        delta_group(
            g, per_group, kq, kk, kv, kg, beta, rel_top, rel_bot, carried, tail,
            readout, local_part, transition, offset,
        )
        relay_slot()
        if g == 0 and exchange:
            for by in range(1, hops + 1):

                @pl.when(place >= by)
                def _():
                    lat_copy_to(by).wait_recv()
                    lat_pass(by).start()

    pos_q = first + iota2((tokens, 1), 0)
    doc_q = jnp.zeros_like(pos_q)
    end = jnp.int32(0)
    for d in range(lengths_ref.shape[1]):
        end = end + lengths_ref[0, d]
        doc_q = doc_q + jnp.where(pos_q >= end, 1, 0)
    for n in range(2):
        q = slice(n * rows, (n + 1) * rows)
        pos_key = pos_q[n * rows : n * rows + 1] - (key_count - rows) + iota2((1, key_count), 1)
        doc_key = jnp.zeros_like(pos_key)
        end = jnp.int32(0)
        for d in range(lengths_ref.shape[1]):
            end = end + lengths_ref[0, d]
            doc_key = doc_key + jnp.where(pos_key >= end, 1, 0)
        bias[n] = jnp.where(
            (pos_key <= pos_q[q]) & (pos_key >= 0) & (doc_key == doc_q[q]), 0.0, masked_score
        )

    lat_copy.wait()
    for by in range(1, hops + 1):

        @pl.when(place >= by)
        def _():
            if exchange:
                lat_pass(by).wait_recv()
            else:
                lat_copy_to(by).wait_recv()

    spare = even.shape[1] - width
    blank = jnp.zeros((tokens, spare), window.dtype)
    for n in range(hops + 1):
        part = slice(n * tokens, (n + 1) * tokens)
        begin = first_key if n == 0 else 0
        part = slice(n * tokens + begin, (n + 1) * tokens)
        even[part] = jnp.concatenate([window[part], blank[begin:]], axis=1)
        odd[part] = jnp.concatenate([blank[begin:], window[part]], axis=1)

    attend = functools.partial(
        attend_step, width=width, first_key=first_key, key_count=key_count, score_scale=score_scale
    )

    def far_copy(n):
        return pltpu.make_async_remote_copy(
            src_ref=far_send.at[n],
            dst_ref=far_recv.at[n],
            send_sem=far_ssem.at[n],
            recv_sem=far_rsem.at[n],
            device_id=partner,
            device_id_type=MESH,
        )

    def project(n):
        return jnp.dot(head_out[...], proj[:, pl.ds(pl.multiple_of(n * CHUNK, CHUNK), CHUNK)],
                       preferred_element_type=jnp.float32)

    thirds = [(t * pieces // 3, (t + 1) * pieces // 3) for t in range(3)]
    far_half = 1 - mine if exchange else 0
    near_half = mine if exchange else 1

    up_copy.wait()
    for step in range(steps):
        mq_copies[step].wait()
        attend(far_half, step, per_step, mq, even, odd, bias, up, head_out)
        relay_slot()
    for copy in proj_copies:
        copy.wait()

    def far_piece(n, _):
        part = project(n).astype(jnp.bfloat16)
        if exchange:
            far_send[n] = part
            far_copy(n).start()
        else:
            mixed_stage[0, :rows, pl.ds(pl.multiple_of(n * CHUNK, CHUNK), CHUNK)] = part
        return 0

    for begin, stop in thirds:
        lax.fori_loop(begin, stop, far_piece, 0)
        relay_slot()
    for step in range(steps):
        attend(near_half, step, per_step, mq, even, odd, bias, up, head_out)
        relay_slot()

    def near_piece(n, _):
        part = project(n)
        at = pl.ds(pl.multiple_of(n * CHUNK, CHUNK), CHUNK)
        if exchange:
            far_copy(n).wait_recv()
            mixed_stage[0, :, at] = (part + far_recv[n].astype(jnp.float32)).astype(jnp.bfloat16)
        else:
            mixed_stage[0, rows:, at] = part.astype(jnp.bfloat16)
        return 0

    for begin, stop in thirds:
        lax.fori_loop(begin, stop, near_piece, 0)
        relay_slot()
    for h in range(heads):
        at = pl.ds(h * state_dim, state_dim)
        kda_stage[0, :, at] = (
            local_part[:, at]
            + jnp.dot(readout[:, at], state_in[h], preferred_element_type=jnp.float32)
        ).astype(kda_stage.dtype)

    for by in range(1, hops + 1):

        @pl.when(place + by < ctx_count)
        def _():
            lat_copy_to(by).wait_send()

        if exchange:

            @pl.when(place >= by)
            def _():
                lat_pass(by).wait_send()

    @pl.when(place + 1 < ctx_count)
    def _():
        for c in range(passes):
            state_copy(c).wait_send()

    if exchange:
        for n in range(pieces):
            far_copy(n).wait_send()


def local(
    kda_query, kda_key, kda_value, log_decay, write_strength, mla_query, latents, value_up,
    out_proj, doc_lengths,
):
    tokens = kda_query.shape[1]
    heads = write_strength.shape[1]
    lanes = kda_query.shape[2]
    state_dim = lanes // heads
    ctx_count = lax.axis_size("ctx")
    head_count = lax.axis_size("head")
    exchange = head_count == 2
    longest = 3 * tokens * ctx_count // 8
    hops = min(ctx_count - 1, -(-(longest - 1) // tokens))
    width = latents.shape[2]
    spare = -width % 128
    model = out_proj.shape[1]
    rows = tokens // 2
    back = -(-(longest - 1) // rows) * rows
    first_key = hops * tokens - back
    need = [min(tokens, back - (by - 1) * tokens) for by in range(1, hops + 1)]
    per_group = math.gcd(heads, 8)
    per_step = math.gcd(heads, 8)
    per_pass = 2
    top = 2 * (tokens // 3)
    wide = 2 * top
    groups, steps, passes, pieces = (
        heads // per_group, heads // per_step, heads // per_pass, model // CHUNK,
    )
    window_rows = (hops + 1) * tokens
    bf16, f32 = jnp.bfloat16, jnp.float32
    vmem = pltpu.VMEM
    dma = pltpu.SemaphoreType.DMA
    scratch = [
        vmem((tokens, lanes), bf16),
        vmem((tokens, lanes), bf16),
        vmem((tokens, lanes), bf16),
        vmem((tokens, lanes), bf16),
        vmem((heads, tokens), f32),
        vmem((tokens, heads * width), bf16),
        vmem((window_rows, width), bf16),
        vmem((window_rows, width + spare), bf16),
        vmem((window_rows, width + spare), bf16),
        vmem(value_up.shape, bf16),
        vmem(out_proj.shape, bf16),
        vmem((top, top), jnp.int32),
        vmem((tokens - top, wide), jnp.int32),
        vmem((tokens, state_dim), f32),
        vmem((tokens, state_dim), f32),
        vmem((groups, tokens, 128), f32),
        vmem((tokens, lanes), bf16),
        vmem((tokens, lanes), f32),
        vmem((heads, state_dim, state_dim), bf16),
        vmem((heads, state_dim, state_dim), f32),
        vmem((heads, state_dim, state_dim), bf16),
        vmem((heads, state_dim, state_dim), bf16),
        vmem((2, rows, back + rows), f32),
        vmem((rows, heads * value_up.shape[2]), bf16),
        vmem((pieces, rows, CHUNK), bf16),
        vmem((pieces, rows, CHUNK), bf16),
        dma((groups, 4)),
        dma((3 + steps,)),
        dma((pieces,)),
        dma((hops,)),
        dma((hops,)),
        dma((hops,)),
        dma((hops,)),
        dma((passes,)),
        dma((passes,)),
        dma((pieces,)),
        dma((pieces,)),
    ]
    anywhere = pl.BlockSpec(memory_space=pl.ANY)
    kda_out, mixed = pl.pallas_call(
        functools.partial(
            layers, hops=hops, need=need, width=width, per_group=per_group, per_step=per_step,
            per_pass=per_pass, first_key=first_key, key_count=back + rows,
            score_scale=1.0 / math.sqrt(NOPE + ROPE), exchange=exchange,
        ),
        in_specs=[pl.BlockSpec(memory_space=pltpu.SMEM)] + [anywhere] * 9,
        out_specs=[pl.BlockSpec(memory_space=pltpu.VMEM)] * 2,
        out_shape=[
            pltpu.VMEM((1, tokens, lanes), bf16),
            pltpu.VMEM((1, rows if exchange else tokens, model), bf16),
        ],
        scratch_shapes=scratch,
        compiler_params=pltpu.CompilerParams(
            vmem_limit_bytes=58 << 20, collective_id=0, has_side_effects=True
        ),
        cost_estimate=pl.CostEstimate(
            flops=10_000_000_000, bytes_accessed=20_000_000, transcendentals=0
        ),
    )(
        doc_lengths, in_place(kda_query), in_place(kda_key), in_place(kda_value),
        in_place(log_decay), in_place(write_strength), in_place(mla_query), in_place(latents),
        in_place(value_up), in_place(out_proj),
    )
    if not exchange:
        mixed = lax.psum_scatter(mixed, "head", scatter_dimension=1, tiled=True)
    return kda_out, mixed


def solution(mesh):
    placed = (
        P(("group", "req"), "ctx", "head"),
        P(("group", "req"), "ctx", "head"),
        P(("group", "req"), "ctx", "head"),
        P(("group", "req"), "ctx", "head"),
        P(("group", "req"), "head", "ctx"),
        P(("group", "req"), "ctx", "head"),
        P(("group", "req"), "ctx", None),
        P("head", None, None),
        P("head", None),
        P(("group", "req"), None),
    )
    return jax.shard_map(
        local,
        mesh=mesh,
        in_specs=placed,
        out_specs=(P(("group", "req"), "ctx", "head"), P(("group", "req"), ("ctx", "head"), None)),
        check_vma=False,
    )
```

```python
import functools
import math

import jax
import jax.numpy as jnp
from jax import lax
from jax.experimental import pallas as pl
from jax.experimental.pallas import tpu as pltpu
from jax.sharding import PartitionSpec as P

ROPE = 64
NOPE = 128
MESH = pl.DeviceIdType.MESH
CHUNK = 256

DELTA_AT = 26
DELTA_TIME = 78
TURN_AT = 107
ATTEND_TIME = 35
PROJECT_TIME = 28
FIRST_PASS = 87
HOP_LATE = 39
PASS_TIME = 14

masked_score = -1e30
ROWS = (((1,), (0,)), ((), ()))
TRANS = (((1,), (1,)), ((), ()))
OVER = (((0,), (0,)), ((), ()))


def in_place(value):
    return pltpu.with_memory_space_constraint(value, pltpu.HBM)


def dot_once(left, right, dims):
    return lax.dot_general(
        left.astype(jnp.bfloat16),
        right.astype(jnp.bfloat16),
        dims,
        preferred_element_type=jnp.float32,
    )


def iota2(shape, axis):
    return lax.broadcasted_iota(jnp.int32, shape, axis)


def delta_setup(lengths_ref, strength_ref, rel_top, rel_bot, carried_ref, tail_ref, beta_ref, first, per_group):
    tokens, state_dim = carried_ref.shape
    top = rel_top.shape[0]
    wide = rel_bot.shape[1]
    bot = tokens - top
    pos_col = first + iota2((tokens, 1), 0)
    pos_row = first + iota2((1, wide), 1)
    doc_col, doc_row = jnp.zeros_like(pos_col), jnp.zeros_like(pos_row)
    prev_doc, last_doc, end = jnp.int32(0), jnp.int32(0), jnp.int32(0)
    for d in range(lengths_ref.shape[1]):
        end = end + lengths_ref[0, d]
        doc_col = doc_col + jnp.where(pos_col >= end, 1, 0)
        doc_row = doc_row + jnp.where(pos_row >= end, 1, 0)
        prev_doc = prev_doc + jnp.where(first - 1 >= end, 1, 0)
        last_doc = last_doc + jnp.where(first + tokens - 1 >= end, 1, 0)
    rel_top[...] = jnp.where(
        doc_col[:top] == doc_row[:, :top], iota2((top, top), 0) - iota2((top, top), 1), -1
    )
    rel_bot[...] = jnp.where(
        (doc_col[top:] == doc_row) & (iota2((bot, wide), 1) < tokens),
        iota2((bot, wide), 0) + top - iota2((bot, wide), 1),
        -1,
    )
    ones = jnp.ones((1, state_dim), jnp.float32)
    carried_ref[...] = jnp.where(doc_col == prev_doc, 1.0, 0.0) * ones
    tail_ref[...] = jnp.where(doc_col == last_doc, 1.0, 0.0) * ones
    heads = strength_ref.shape[0]
    padded = jnp.concatenate(
        [strength_ref[...], jnp.zeros((heads, wide - tokens), jnp.float32)], axis=1
    )
    padded = jnp.concatenate([padded, jnp.zeros((128 - heads, wide), jnp.float32)], axis=0)
    turned = jnp.transpose(padded)[:tokens]
    for g in range(heads // per_group):
        beta_ref[g] = turned if g == 0 else pltpu.roll(turned, 128 - g * per_group, 1)


def packed_inverse(pack):
    lane = iota2((1, 128), 1)
    piece = pack[0:16]
    for b in range(1, 4):
        piece = jnp.where((lane % 64) // 16 == b, pack[16 * b : 16 * b + 16], piece)
    row16, col16 = iota2((16, 128), 0), iota2((16, 128), 1) % 16
    inv = jnp.where((row16 // 2 == col16 // 2) & (row16 > col16), -piece, 0.0)
    yield
    for width, size in ((2, 16), (4, 16), (8, 16), (16, 32), (32, 64)):
        if size == 32:
            piece = jnp.where((lane % 64) // 32 == 0, pack[0:32], pack[32:64])
        elif size == 64:
            piece = pack
        if width == size // 2 and size > 16:
            inv = jnp.concatenate(
                [
                    jnp.where(lane % size < width, inv, 0.0),
                    jnp.where(lane % size >= width, inv, 0.0),
                ],
                axis=0,
            )
        row, col = iota2((size, 128), 0), iota2((size, 128), 1) % size
        corner = (row // (2 * width) == col // (2 * width)) & (row // width > col // width)
        part = jnp.where(corner, piece, 0.0)
        left = part + dot_once(inv, spread(part, size), ROWS)
        yield
        inv = inv - (left + dot_once(left, spread(inv, size), ROWS))
        yield
    yield inv


def spread(cells, size):
    copies = 128 // size
    own = iota2((128, 128), 0) // size == iota2((128, 128), 1) // size
    return jnp.where(own, jnp.concatenate([cells] * copies, axis=0), 0.0).astype(jnp.bfloat16)


def together(makers):
    done = []
    while True:
        step = [next(m) for m in makers]
        if step[0] is not None:
            return step


def delta_group(
    g, per_group, query_ref, key_ref, value_ref, decay_ref, beta_ref, rel_top, rel_bot,
    carried_ref, tail_ref, readout_ref, local_ref, transition_ref, offset_ref,
    scored, inverted, done,
):
    tokens, state_dim = carried_ref.shape
    top = rel_top.shape[0]
    half = top // 2
    heads = range(per_group)
    inclusive = jnp.where(
        iota2((tokens, tokens), 0) >= iota2((tokens, tokens), 1), 1.0, 0.0
    ).astype(jnp.bfloat16)
    lane = iota2((1, 128), 1)
    at = [
        pl.ds(pl.multiple_of((g * per_group + h) * state_dim, state_dim), state_dim) for h in heads
    ]
    summed = []
    for h in range(0, per_group, 2):
        both = pl.ds(
            pl.multiple_of((g * per_group + h) * state_dim, 2 * state_dim), 2 * state_dim
        )
        pair = jnp.dot(inclusive, decay_ref[:, both], preferred_element_type=jnp.float32)
        summed += [pair[:, :state_dim], pair[:, state_dim:]]
    lower_top, lower_bot, attend_top, attend_bot = [], [], [], []
    right_keys, read_query, key_decay, kept, rights = [], [], [], [], []
    for h in heads:
        s = summed[h]
        query = query_ref[:, at[h]].astype(jnp.float32)
        key = key_ref[:, at[h]].astype(jnp.float32)
        beta = beta_ref[g, :, h : h + 1]
        query = query * lax.rsqrt(jnp.sum(query * query, axis=1, keepdims=True) + 1e-06)
        key = key * lax.rsqrt(jnp.sum(key * key, axis=1, keepdims=True) + 1e-06)
        written = key * beta
        mid, start, last = s[half - 1 : half], s[top - 1 : top], s[tokens - 1 : tokens]
        fall_top, fall_bot = jnp.exp(s[:top] - mid), jnp.exp(s[top:] - start)
        lift_top, lift_bot = jnp.exp(mid - s[:top]), jnp.exp(start - s[top:])
        to_mid, to_start, mid_start = jnp.exp(mid), jnp.exp(start), jnp.exp(start - mid)
        key_top, key_bot = written[:top] * fall_top, written[top:] * fall_bot
        query_top, query_bot = query[:top] * fall_top, query[top:] * fall_bot
        raised_top = key[:top] * lift_top
        raised_all = jnp.concatenate([raised_top * mid_start, key[top:] * lift_bot], axis=0)
        both_top = dot_once(
            jnp.concatenate([key_top, query_top], axis=0), raised_top, TRANS
        )
        both_bot = dot_once(
            jnp.concatenate([key_bot, query_bot], axis=0),
            jnp.concatenate([raised_all, jnp.zeros((half, state_dim), jnp.float32)], axis=0),
            TRANS,
        )
        lower_top.append(jnp.where(rel_top[...] > 0, both_top[:top], 0.0))
        attend_top.append(jnp.where(rel_top[...] >= 0, both_top[top:], 0.0).astype(jnp.bfloat16))
        lower_bot.append(jnp.where(rel_bot[...] > 0, both_bot[:half], 0.0))
        attend_bot.append(
            jnp.where(rel_bot[...] >= 0, both_bot[half:], 0.0).astype(jnp.bfloat16)
        )
        carried = carried_ref[...]
        grown = jnp.concatenate([key_top * to_mid, key_bot * to_start], axis=0) * carried
        read_query.append(
            jnp.concatenate([query_top * to_mid, query_bot * to_start], axis=0) * carried
        )
        key_decay.append((raised_all * jnp.exp(last - start) * tail_ref[...]).astype(jnp.bfloat16))
        kept.append(jnp.exp(last) * carried[tokens - 1 : tokens])
        rights.append(
            jnp.concatenate([grown, value_ref[:, at[h]].astype(jnp.float32) * beta], axis=1)
        )
    done = scored(done)
    makers = [
        packed_inverse(jnp.where(lane < half, lower_top[h][:half], lower_top[h][half:]))
        for h in heads
    ]
    makers += [
        packed_inverse(
            jnp.where(
                lane < half,
                lower_bot[h][:, top:],
                pltpu.roll(lower_bot[h + 1][:, top:], half, 1),
            )
        )
        for h in range(0, per_group, 2)
    ]
    inverses = together(makers)
    done = inverted(done)
    firsts, seconds, tops, wholes = [], [], [], []
    for h in heads:
        right = rights[h]
        inv = jnp.where(lane < half, inverses[h], 0.0)
        firsts.append(right[:half] + dot_once(inv, right[:top], ROWS))
    for h in heads:
        across = jnp.where(lane < half, lower_top[h][half:], 0.0)
        seconds.append(
            rights[h][half:top]
            - dot_once(across, jnp.concatenate([firsts[h]] * 2, axis=0), ROWS)
        )
    for h in heads:
        inv = jnp.where(lane >= half, inverses[h], 0.0)
        tops.append(
            jnp.concatenate(
                [
                    firsts[h],
                    seconds[h] + dot_once(inv, jnp.concatenate([seconds[h]] * 2, axis=0), ROWS),
                ],
                axis=0,
            ).astype(jnp.bfloat16)
        )
    thirds = [
        rights[h][top:] - dot_once(lower_bot[h][:, :top], tops[h], ROWS) for h in heads
    ]
    for h in heads:
        inv = inverses[per_group + h // 2]
        inv = jnp.where(lane < half, inv, 0.0) if h % 2 == 0 else jnp.where(lane >= half, inv, 0.0)
        third = thirds[h] + dot_once(inv, jnp.concatenate([thirds[h]] * 2, axis=0), ROWS)
        wholes.append(jnp.concatenate([tops[h], third.astype(jnp.bfloat16)], axis=0))
    eye = iota2((state_dim, state_dim), 0) == iota2((state_dim, state_dim), 1)
    for h in heads:
        moved = dot_once(key_decay[h], wholes[h], OVER)
        head = g * per_group + h
        transition_ref[head] = (
            jnp.where(eye, kept[h], 0.0) - moved[:, :state_dim]
        ).astype(transition_ref.dtype)
        offset_ref[head] = moved[:, state_dim:]
    for h in heads:
        read = dot_once(attend_top[h], tops[h], ROWS)
        readout_ref[:top, at[h]] = (read_query[h][:top] - read[:, :state_dim]).astype(
            readout_ref.dtype
        )
        local_ref[:top, at[h]] = read[:, state_dim:]
        read = dot_once(attend_bot[h][:, :tokens], wholes[h], ROWS)
        readout_ref[top:, at[h]] = (read_query[h][top:] - read[:, :state_dim]).astype(
            readout_ref.dtype
        )
        local_ref[top:, at[h]] = read[:, state_dim:]
    return done


def attend_step(
    half, step, group, query_ref, even_ref, odd_ref, bias_ref, up_ref, out_ref,
    *, width, first_key, key_count, score_scale,
):
    rows = out_ref.shape[0]
    wide = even_ref.shape[1]
    lat_dim, vhead = up_ref.shape[1:]
    pairs = group // 2
    keys = pl.ds(pl.multiple_of(half * rows + first_key, math.gcd(rows, first_key)), key_count)
    own = pl.ds(pl.multiple_of(half * rows, rows), rows)
    bias = bias_ref[half]
    contexts = []
    for key_ref, skip in ((even_ref, 0), (odd_ref, 2 * width - wide)):
        stacked = []
        for p in range(pairs):
            begin = (step * group + 2 * p) * width + skip
            stacked.append(query_ref[own, pl.ds(pl.multiple_of(begin, 128), wide)])
        query = jnp.concatenate(stacked, axis=0) if pairs > 1 else stacked[0]
        scores = lax.dot_general(
            query, key_ref[keys, :], TRANS, preferred_element_type=jnp.float32
        )
        scores = scores.reshape(pairs, rows, key_count) * score_scale + bias[None]
        exponent = jnp.exp(scores - jnp.max(scores, axis=2, keepdims=True))
        exponent = exponent.reshape(pairs * rows, key_count)
        row_total = jnp.sum(exponent, axis=1, keepdims=True)
        weighted = jnp.dot(
            exponent.astype(jnp.bfloat16),
            even_ref[keys, :lat_dim],
            preferred_element_type=jnp.float32,
        )
        contexts.append((weighted / row_total).astype(jnp.bfloat16))
    for p in range(pairs):
        for parity in range(2):
            head = step * group + 2 * p + parity
            out_ref[:, pl.ds(pl.multiple_of(head * vhead, vhead), vhead)] = jnp.dot(
                contexts[parity][p * rows : (p + 1) * rows],
                up_ref[head],
                preferred_element_type=jnp.float32,
            ).astype(jnp.bfloat16)


def layers(
    lengths_hbm, kq_hbm, kk_hbm, kv_hbm, kg_hbm, strength_hbm, mq_hbm, lat_hbm, up_hbm, proj_hbm,
    kda_stage, mixed_stage,
    lengths_ref, kq, kk, kv, kg, strength, mq, window, even, odd, up, proj,
    rel_top, rel_bot, carried, tail, beta, readout, local_part, transition, offset,
    state_out, state_in, bias, head_out, far_send, far_recv, near_part,
    kda_sem, load_sem, lat_send, lat_recv, pass_send, pass_recv,
    state_send, state_recv, far_ssem, far_rsem,
    *, hops, need, width, per_group, per_step, per_pass, first_key, key_count, score_scale, exchange,
):
    tokens, lanes = kq.shape
    heads = strength.shape[0]
    state_dim = lanes // heads
    groups = heads // per_group
    steps = heads // per_step
    passes = heads // per_pass
    rows = tokens // 2
    ctx_count = lax.axis_size("ctx")
    place = lax.axis_index("ctx")
    mine = lax.axis_index("head")
    model = proj.shape[1]
    pieces = model // CHUNK
    first = place * tokens

    def up_by(by):
        return {"ctx": place + by}

    partner = {"head": 1 - mine}

    def load(source, target, sem):
        return pltpu.make_async_copy(source, target, sem)

    def kda_loads(g):
        part = pl.ds(pl.multiple_of(g * per_group * state_dim, state_dim), per_group * state_dim)
        return [
            load(source.at[0, :, part], target.at[:, part], kda_sem.at[g, n])
            for n, (source, target) in enumerate(
                ((kg_hbm, kg), (kq_hbm, kq), (kk_hbm, kk), (kv_hbm, kv))
            )
        ]

    strength_copy = load(strength_hbm.at[0], strength, load_sem.at[0])
    lat_copy = load(lat_hbm.at[0], window, load_sem.at[1])
    mq_copy = load(mq_hbm.at[0], mq, load_sem.at[2])
    up_copy = load(up_hbm, up, load_sem.at[3])
    proj_copy = load(proj_hbm, proj, load_sem.at[4])
    lengths_copy = load(lengths_hbm, lengths_ref, load_sem.at[5])

    barrier = pltpu.get_barrier_semaphore()
    halved = exchange and hops == 2 and need == [tokens, rows]
    peers = jnp.int32(0)
    for by in range(1, 2 if halved else hops + 1):
        for sign in (1, -1):
            there = place + sign * by
            known = (there >= 0) & (there < ctx_count)
            peers = peers + jnp.where(known, 1, 0)

            @pl.when(known)
            def _():
                pl.semaphore_signal(
                    barrier, inc=1, device_id={"ctx": there}, device_id_type=MESH
                )

    if exchange:
        pl.semaphore_signal(barrier, inc=1, device_id=partner, device_id_type=MESH)
        peers = peers + 1

    lat_copy.start()
    lengths_copy.start()
    strength_copy.start()
    for g in range(groups):
        for copy in kda_loads(g):
            copy.start()


    def lat_copy_to(by):
        count = rows if halved else need[by - 1]
        begin = pl.multiple_of(rows * mine, rows) if halved else tokens - count
        behind = by - 1 if halved else 0
        return pltpu.make_async_remote_copy(
            src_ref=even.at[pl.ds(begin + (hops - behind) * tokens, count)],
            dst_ref=even.at[pl.ds(begin + (hops - by) * tokens, count)],
            send_sem=lat_send.at[by - 1],
            recv_sem=lat_recv.at[by - 1],
            device_id=up_by(1 if halved else by),
            device_id_type=MESH,
        )

    def lat_pass(by):
        begin = pl.multiple_of(rows * mine, rows)
        region = even.at[pl.ds(begin + (hops - by) * tokens, rows)]
        return pltpu.make_async_remote_copy(
            src_ref=region,
            dst_ref=even.at[pl.ds(begin + (hops - by) * tokens, rows)],
            send_sem=pass_send.at[by - 1],
            recv_sem=pass_recv.at[by - 1],
            device_id=partner,
            device_id_type=MESH,
        )

    direct = range(1, 2 if halved else hops + 1)
    upper = mine == 1
    sends_on = upper & (place >= 1) & (place + 1 < ctx_count)
    far_comes = place >= 2

    blank = jnp.zeros((tokens, even.shape[1] - width), even.dtype)
    lat_copy.wait()
    even[hops * tokens :] = jnp.concatenate([window[...], blank], axis=1)
    pl.semaphore_wait(barrier, peers)
    for by in direct:

        @pl.when(place + by < ctx_count)
        def _():
            lat_copy_to(by).start()

    mq_copy.start()
    up_copy.start()
    proj_copy.start()

    def state_copy(c):
        part = pl.ds(c * per_pass, per_pass)
        return pltpu.make_async_remote_copy(
            src_ref=state_out.at[part],
            dst_ref=state_in.at[part],
            send_sem=state_send.at[c],
            recv_sem=state_recv.at[c],
            device_id=up_by(1),
            device_id_type=MESH,
        )

    def relay(c, _):
        @pl.when(place > 0)
        def _():
            state_copy(c).wait_recv()

        @pl.when(place == 0)
        def _():
            for n in range(per_pass):
                head = c * per_pass + n
                state_out[head] = offset[head].astype(state_out.dtype)

        @pl.when((place > 0) & (place + 1 < ctx_count))
        def _():
            for n in range(per_pass):
                head = c * per_pass + n
                state_out[head] = (
                    offset[head]
                    + jnp.dot(
                        transition[head], state_in[head], preferred_element_type=jnp.float32
                    )
                ).astype(state_out.dtype)

        @pl.when(place + 1 < ctx_count)
        def _():
            state_copy(c).start()

        return 0

    passes_group = passes // groups

    def relay_slot(time, ready, before):
        due = (time - FIRST_PASS - HOP_LATE * (place - 1)) // PASS_TIME + 1
        due = jnp.where(place == 0, ready, jnp.where(place == ctx_count - 1, 0, due))
        after = jnp.maximum(before, jnp.minimum(due, passes))
        lax.fori_loop(before, after, relay, 0)
        return after

    for by in range(1, hops + 1):

        @pl.when(place < by)
        def _():
            stop = (hops - by + 1) * tokens
            even[stop - need[by - 1] : stop] = jnp.zeros(
                (need[by - 1], even.shape[1]), even.dtype
            )

    lengths_copy.wait()
    strength_copy.wait()
    delta_setup(
        lengths_ref, strength, rel_top, rel_bot, carried, tail, beta, first, per_group
    )
    pos_q = first + iota2((tokens, 1), 0)
    for n in range(2):
        q = slice(n * rows, (n + 1) * rows)
        pos_key = pos_q[n * rows : n * rows + 1] - (key_count - rows) + iota2((1, key_count), 1)
        doc_q, doc_key = jnp.zeros((rows, 1), jnp.int32), jnp.zeros_like(pos_key)
        end = jnp.int32(0)
        for d in range(lengths_ref.shape[1]):
            end = end + lengths_ref[0, d]
            doc_q = doc_q + jnp.where(pos_q[q] >= end, 1, 0)
            doc_key = doc_key + jnp.where(pos_key >= end, 1, 0)
        bias[n] = jnp.where(
            (pos_key <= pos_q[q]) & (pos_key >= 0) & (doc_key == doc_q), 0.0, masked_score
        )

    def pass_latents():
        @pl.when(place >= 1)
        def _():
            lat_copy_to(1).wait_recv()

        @pl.when(sends_on)
        def _():
            lat_copy_to(2).start()

        @pl.when(place >= 1)
        def _():
            lat_pass(1).start()

    def delta_step(g, done):
        for copy in kda_loads(g):
            copy.wait()
        begin = DELTA_AT + DELTA_TIME * g // groups

        def scored(done):
            return relay_slot(begin + DELTA_TIME * 2 // (5 * groups), passes_group * g, done)

        def inverted(done):
            return relay_slot(begin + DELTA_TIME * 3 // (4 * groups), passes_group * g, done)

        done = delta_group(
            g, per_group, kq, kk, kv, kg, beta, rel_top, rel_bot, carried, tail,
            readout, local_part, transition, offset, scored, inverted, done,
        )
        done = relay_slot(begin + DELTA_TIME // groups, passes_group * (g + 1), done)
        if halved:
            pl.when(g == 0)(pass_latents)

        return done

    done = lax.fori_loop(0, groups, delta_step, jnp.int32(0))

    def shifted(n):
        begin = first_key if n == 0 else 0
        part = slice(n * tokens + begin, (n + 1) * tokens)
        odd[part] = jnp.concatenate([blank[begin:], even[part][:, :width]], axis=1)

    if halved:

        @pl.when(place >= 1)
        def _():
            lat_pass(1).wait_recv()

        @pl.when(upper & far_comes)
        def _():
            lat_copy_to(2).wait_recv()
            lat_pass(2).start()

        @pl.when(upper)
        def _():
            shifted(0)

    else:
        for by in direct:

            @pl.when(place >= by)
            def _():
                lat_copy_to(by).wait_recv()

            shifted(hops - by)

    def last_latents():
        @pl.when(far_comes)
        def _():
            lat_pass(2).wait_recv()

        shifted(0)

    for n in range(1 if halved else hops, hops + 1):
        shifted(n)

    def far_copy(n):
        return pltpu.make_async_remote_copy(
            src_ref=far_send.at[n],
            dst_ref=far_recv.at[n],
            send_sem=far_ssem.at[n],
            recv_sem=far_rsem.at[n],
            device_id=partner,
            device_id_type=MESH,
        )

    far_half = 1 - mine if exchange else 0
    near_half = mine if exchange else 1
    up_copy.wait()
    mq_copy.wait()

    def attention(turn, done):
        half = jnp.where(turn == 0, far_half, near_half)
        if halved:
            pl.when((turn == 1) & (mine == 0))(last_latents)
        time = TURN_AT + turn * (ATTEND_TIME + PROJECT_TIME)

        def attend_turn(step, done):
            attend_step(
                half, step, per_step, mq, even, odd, bias, up, head_out,
                width=width, first_key=first_key, key_count=key_count, score_scale=score_scale,
            )
            return relay_slot(time + ATTEND_TIME * (step + 1) // steps, passes, done)

        done = lax.fori_loop(0, steps, attend_turn, done)

        @pl.when(turn == 0)
        def _():
            proj_copy.wait()

        def project(n, done):
            part = jnp.dot(
                head_out[...],
                proj[:, pl.ds(pl.multiple_of(n * CHUNK, CHUNK), CHUNK)],
                preferred_element_type=jnp.float32,
            )

            @pl.when(turn == 0)
            def _():
                far_send[n] = part.astype(jnp.bfloat16)
                if exchange:
                    far_copy(n).start()

            @pl.when(turn == 1)
            def _():
                near_part[n] = part

            return relay_slot(
                time + ATTEND_TIME + PROJECT_TIME * (n + 1) // pieces, passes, done
            )

        return lax.fori_loop(0, pieces, project, done)

    done = lax.fori_loop(0, 2, attention, done)

    def read_heads(c, _):
        @pl.when(c >= done)
        def _():
            relay(c, 0)

        for n in range(per_pass):
            head = c * per_pass + n
            at = pl.ds(pl.multiple_of(head * state_dim, state_dim), state_dim)

            @pl.when(place > 0)
            def _():
                kda_stage[0, :, at] = (
                    local_part[:, at]
                    + jnp.dot(readout[:, at], state_in[head], preferred_element_type=jnp.float32)
                ).astype(kda_stage.dtype)

            @pl.when(place == 0)
            def _():
                kda_stage[0, :, at] = local_part[:, at].astype(kda_stage.dtype)

        return 0

    lax.fori_loop(0, passes, read_heads, 0)

    def mix(n, _):
        at = pl.ds(pl.multiple_of(n * CHUNK, CHUNK), CHUNK)
        if exchange:
            far_copy(n).wait_recv()
            mixed_stage[0, :, at] = (near_part[n] + far_recv[n].astype(jnp.float32)).astype(
                jnp.bfloat16
            )
        else:
            mixed_stage[0, :rows, at] = far_send[n]
            mixed_stage[0, rows:, at] = near_part[n].astype(jnp.bfloat16)
        return 0

    lax.fori_loop(0, pieces, mix, 0)

    for by in direct:

        @pl.when(place + by < ctx_count)
        def _():
            lat_copy_to(by).wait_send()

    if halved:

        @pl.when(place >= 1)
        def _():
            lat_pass(1).wait_send()

        @pl.when(sends_on)
        def _():
            lat_copy_to(2).wait_send()

        @pl.when(upper & far_comes)
        def _():
            lat_pass(2).wait_send()

    @pl.when(place + 1 < ctx_count)
    def _():
        for c in range(passes):
            state_copy(c).wait_send()

    if exchange:
        for n in range(pieces):
            far_copy(n).wait_send()


def local(
    kda_query, kda_key, kda_value, log_decay, write_strength, mla_query, latents, value_up,
    out_proj, doc_lengths,
):
    tokens = kda_query.shape[1]
    heads = write_strength.shape[1]
    lanes = kda_query.shape[2]
    state_dim = lanes // heads
    ctx_count = lax.axis_size("ctx")
    head_count = lax.axis_size("head")
    exchange = head_count == 2
    longest = 3 * tokens * ctx_count // 8
    hops = min(ctx_count - 1, -(-(longest - 1) // tokens))
    width = latents.shape[2]
    spare = -width % 128
    model = out_proj.shape[1]
    rows = tokens // 2
    back = -(-(longest - 1) // rows) * rows
    first_key = hops * tokens - back
    need = [min(tokens, back - (by - 1) * tokens) for by in range(1, hops + 1)]
    per_group = math.gcd(heads, 8)
    per_step = math.gcd(heads, 8)
    per_pass = 2
    top = 2 * (tokens // 3)
    wide = 2 * top
    groups, steps, passes, pieces = (
        heads // per_group, heads // per_step, heads // per_pass, model // CHUNK,
    )
    window_rows = (hops + 1) * tokens
    bf16, f32 = jnp.bfloat16, jnp.float32
    vmem = pltpu.VMEM
    dma = pltpu.SemaphoreType.DMA
    scratch = [
        pltpu.SMEM(doc_lengths.shape, jnp.int32),
        vmem((tokens, lanes), bf16),
        vmem((tokens, lanes), bf16),
        vmem((tokens, lanes), bf16),
        vmem((tokens, lanes), bf16),
        vmem((heads, tokens), f32),
        vmem((tokens, heads * width), bf16),
        vmem((tokens, width), bf16),
        vmem((window_rows, width + spare), bf16),
        vmem((window_rows, width + spare), bf16),
        vmem(value_up.shape, bf16),
        vmem(out_proj.shape, bf16),
        vmem((top, top), jnp.int32),
        vmem((tokens - top, wide), jnp.int32),
        vmem((tokens, state_dim), f32),
        vmem((tokens, state_dim), f32),
        vmem((groups, tokens, 128), f32),
        vmem((tokens, lanes), bf16),
        vmem((tokens, lanes), f32),
        vmem((heads, state_dim, state_dim), bf16),
        vmem((heads, state_dim, state_dim), f32),
        vmem((heads, state_dim, state_dim), bf16),
        vmem((heads, state_dim, state_dim), bf16),
        vmem((2, rows, back + rows), f32),
        vmem((rows, heads * value_up.shape[2]), bf16),
        vmem((pieces, rows, CHUNK), bf16),
        vmem((pieces, rows, CHUNK), bf16),
        vmem((pieces, rows, CHUNK), f32),
        dma((groups, 4)),
        dma((6,)),
        dma((hops,)),
        dma((hops,)),
        dma((hops,)),
        dma((hops,)),
        dma((passes,)),
        dma((passes,)),
        dma((pieces,)),
        dma((pieces,)),
    ]
    anywhere = pl.BlockSpec(memory_space=pl.ANY)
    kda_out, mixed = pl.pallas_call(
        functools.partial(
            layers, hops=hops, need=need, width=width, per_group=per_group, per_step=per_step,
            per_pass=per_pass, first_key=first_key, key_count=back + rows,
            score_scale=1.0 / math.sqrt(NOPE + ROPE), exchange=exchange,
        ),
        in_specs=[anywhere] * 10,
        out_specs=[pl.BlockSpec(memory_space=pltpu.VMEM)] * 2,
        out_shape=[
            pltpu.VMEM((1, tokens, lanes), bf16),
            pltpu.VMEM((1, rows if exchange else tokens, model), bf16),
        ],
        scratch_shapes=scratch,
        compiler_params=pltpu.CompilerParams(
            vmem_limit_bytes=58 << 20, collective_id=0, has_side_effects=True
        ),
        cost_estimate=pl.CostEstimate(
            flops=10_000_000_000, bytes_accessed=20_000_000, transcendentals=0
        ),
    )(
        in_place(doc_lengths), in_place(kda_query), in_place(kda_key), in_place(kda_value),
        in_place(log_decay), in_place(write_strength), in_place(mla_query), in_place(latents),
        in_place(value_up), in_place(out_proj),
    )
    if not exchange:
        mixed = lax.psum_scatter(mixed, "head", scatter_dimension=1, tiled=True)
    return kda_out, mixed


def solution(mesh):
    placed = (
        P(("group", "req"), "ctx", "head"),
        P(("group", "req"), "ctx", "head"),
        P(("group", "req"), "ctx", "head"),
        P(("group", "req"), "ctx", "head"),
        P(("group", "req"), "head", "ctx"),
        P(("group", "req"), "ctx", "head"),
        P(("group", "req"), "ctx", None),
        P("head", None, None),
        P("head", None),
        P(("group", "req"), None),
    )
    return jax.shard_map(
        local,
        mesh=mesh,
        in_specs=placed,
        out_specs=(P(("group", "req"), "ctx", "head"), P(("group", "req"), ("ctx", "head"), None)),
        check_vma=False,
    )
```

```python
import functools
import math

import jax
import jax.numpy as jnp
from jax import lax
from jax.experimental import pallas as pl
from jax.experimental.pallas import tpu as pltpu
from jax.sharding import PartitionSpec as P

ROPE = 64
NOPE = 128
MESH = pl.DeviceIdType.MESH
CHUNK = 256

DELTA_AT = 26
DELTA_TIME = 78
TURN_AT = 107
ATTEND_TIME = 35
PROJECT_TIME = 28
FIRST_PASS = 87
HOP_LATE = 39
PASS_TIME = 14

masked_score = -1e30
ROWS = (((1,), (0,)), ((), ()))
TRANS = (((1,), (1,)), ((), ()))
OVER = (((0,), (0,)), ((), ()))


def in_place(value):
    return pltpu.with_memory_space_constraint(value, pltpu.HBM)


def dot_once(left, right, dims):
    return lax.dot_general(
        left.astype(jnp.bfloat16),
        right.astype(jnp.bfloat16),
        dims,
        preferred_element_type=jnp.float32,
    )


def iota2(shape, axis):
    return lax.broadcasted_iota(jnp.int32, shape, axis)


def delta_setup(lengths_ref, strength_ref, rel_top, rel_bot, carried_ref, tail_ref, beta_ref, first, per_group):
    tokens, state_dim = carried_ref.shape
    top = rel_top.shape[0]
    wide = rel_bot.shape[1]
    bot = tokens - top
    pos_col = first + iota2((tokens, 1), 0)
    pos_row = first + iota2((1, wide), 1)
    doc_col, doc_row = jnp.zeros_like(pos_col), jnp.zeros_like(pos_row)
    prev_doc, last_doc, end = jnp.int32(0), jnp.int32(0), jnp.int32(0)
    for d in range(lengths_ref.shape[1]):
        end = end + lengths_ref[0, d]
        doc_col = doc_col + jnp.where(pos_col >= end, 1, 0)
        doc_row = doc_row + jnp.where(pos_row >= end, 1, 0)
        prev_doc = prev_doc + jnp.where(first - 1 >= end, 1, 0)
        last_doc = last_doc + jnp.where(first + tokens - 1 >= end, 1, 0)
    rel_top[...] = jnp.where(
        doc_col[:top] == doc_row[:, :top], iota2((top, top), 0) - iota2((top, top), 1), -1
    )
    rel_bot[...] = jnp.where(
        (doc_col[top:] == doc_row) & (iota2((bot, wide), 1) < tokens),
        iota2((bot, wide), 0) + top - iota2((bot, wide), 1),
        -1,
    )
    ones = jnp.ones((1, state_dim), jnp.float32)
    carried_ref[...] = jnp.where(doc_col == prev_doc, 1.0, 0.0) * ones
    tail_ref[...] = jnp.where(doc_col == last_doc, 1.0, 0.0) * ones
    heads = strength_ref.shape[0]
    padded = jnp.concatenate(
        [strength_ref[...], jnp.zeros((heads, wide - tokens), jnp.float32)], axis=1
    )
    padded = jnp.concatenate([padded, jnp.zeros((128 - heads, wide), jnp.float32)], axis=0)
    turned = jnp.transpose(padded)[:tokens]
    for g in range(heads // per_group):
        beta_ref[g] = turned if g == 0 else pltpu.roll(turned, 128 - g * per_group, 1)


def packed_inverse(pack):
    lane = iota2((1, 128), 1)
    piece = pack[0:16]
    for b in range(1, 4):
        piece = jnp.where((lane % 64) // 16 == b, pack[16 * b : 16 * b + 16], piece)
    row16, col16 = iota2((16, 128), 0), iota2((16, 128), 1) % 16
    inv = jnp.where((row16 // 2 == col16 // 2) & (row16 > col16), -piece, 0.0)
    yield
    for width, size in ((2, 16), (4, 16), (8, 16), (16, 32), (32, 64)):
        if size == 32:
            piece = jnp.where((lane % 64) // 32 == 0, pack[0:32], pack[32:64])
        elif size == 64:
            piece = pack
        if width == size // 2 and size > 16:
            inv = jnp.concatenate(
                [
                    jnp.where(lane % size < width, inv, 0.0),
                    jnp.where(lane % size >= width, inv, 0.0),
                ],
                axis=0,
            )
        row, col = iota2((size, 128), 0), iota2((size, 128), 1) % size
        corner = (row // (2 * width) == col // (2 * width)) & (row // width > col // width)
        part = jnp.where(corner, piece, 0.0)
        left = part + dot_once(inv, spread(part, size), ROWS)
        yield
        inv = inv - (left + dot_once(left, spread(inv, size), ROWS))
        yield
    yield inv


def spread(cells, size):
    copies = 128 // size
    own = iota2((128, 128), 0) // size == iota2((128, 128), 1) // size
    return jnp.where(own, jnp.concatenate([cells] * copies, axis=0), 0.0).astype(jnp.bfloat16)


def together(makers):
    done = []
    while True:
        step = [next(m) for m in makers]
        if step[0] is not None:
            return step


def delta_group(
    g, per_group, query_ref, key_ref, value_ref, decay_ref, beta_ref, rel_top, rel_bot,
    carried_ref, tail_ref, readout_ref, local_ref, transition_ref, offset_ref,
    scored, inverted, done,
):
    tokens, state_dim = carried_ref.shape
    top = rel_top.shape[0]
    half = top // 2
    heads = range(per_group)
    inclusive = jnp.where(
        iota2((tokens, tokens), 0) >= iota2((tokens, tokens), 1), 1.0, 0.0
    ).astype(jnp.bfloat16)
    lane = iota2((1, 128), 1)
    at = [
        pl.ds(pl.multiple_of((g * per_group + h) * state_dim, state_dim), state_dim) for h in heads
    ]
    summed = []
    for h in range(0, per_group, 2):
        both = pl.ds(
            pl.multiple_of((g * per_group + h) * state_dim, 2 * state_dim), 2 * state_dim
        )
        pair = jnp.dot(inclusive, decay_ref[:, both], preferred_element_type=jnp.float32)
        summed += [pair[:, :state_dim], pair[:, state_dim:]]
    lower_top, lower_bot, attend_top, attend_bot = [], [], [], []
    right_keys, read_query, key_decay, kept, rights = [], [], [], [], []
    for h in heads:
        s = summed[h]
        query = query_ref[:, at[h]].astype(jnp.float32)
        key = key_ref[:, at[h]].astype(jnp.float32)
        beta = beta_ref[g, :, h : h + 1]
        query = query * lax.rsqrt(jnp.sum(query * query, axis=1, keepdims=True) + 1e-06)
        key = key * lax.rsqrt(jnp.sum(key * key, axis=1, keepdims=True) + 1e-06)
        written = key * beta
        mid, start, last = s[half - 1 : half], s[top - 1 : top], s[tokens - 1 : tokens]
        fall_top, fall_bot = jnp.exp(s[:top] - mid), jnp.exp(s[top:] - start)
        lift_top, lift_bot = jnp.exp(mid - s[:top]), jnp.exp(start - s[top:])
        to_mid, to_start, mid_start = jnp.exp(mid), jnp.exp(start), jnp.exp(start - mid)
        key_top, key_bot = written[:top] * fall_top, written[top:] * fall_bot
        query_top, query_bot = query[:top] * fall_top, query[top:] * fall_bot
        raised_top = key[:top] * lift_top
        raised_all = jnp.concatenate([raised_top * mid_start, key[top:] * lift_bot], axis=0)
        both_top = dot_once(
            jnp.concatenate([key_top, query_top], axis=0), raised_top, TRANS
        )
        both_bot = dot_once(
            jnp.concatenate([key_bot, query_bot], axis=0),
            jnp.concatenate([raised_all, jnp.zeros((half, state_dim), jnp.float32)], axis=0),
            TRANS,
        )
        lower_top.append(jnp.where(rel_top[...] > 0, both_top[:top], 0.0))
        attend_top.append(jnp.where(rel_top[...] >= 0, both_top[top:], 0.0).astype(jnp.bfloat16))
        lower_bot.append(jnp.where(rel_bot[...] > 0, both_bot[:half], 0.0))
        attend_bot.append(
            jnp.where(rel_bot[...] >= 0, both_bot[half:], 0.0).astype(jnp.bfloat16)
        )
        carried = carried_ref[...]
        grown = jnp.concatenate([key_top * to_mid, key_bot * to_start], axis=0) * carried
        read_query.append(
            jnp.concatenate([query_top * to_mid, query_bot * to_start], axis=0) * carried
        )
        key_decay.append((raised_all * jnp.exp(last - start) * tail_ref[...]).astype(jnp.bfloat16))
        kept.append(jnp.exp(last) * carried[tokens - 1 : tokens])
        rights.append(
            jnp.concatenate([grown, value_ref[:, at[h]].astype(jnp.float32) * beta], axis=1)
        )
    done = scored(done)
    makers = [
        packed_inverse(jnp.where(lane < half, lower_top[h][:half], lower_top[h][half:]))
        for h in heads
    ]
    makers += [
        packed_inverse(
            jnp.where(
                lane < half,
                lower_bot[h][:, top:],
                pltpu.roll(lower_bot[h + 1][:, top:], half, 1),
            )
        )
        for h in range(0, per_group, 2)
    ]
    inverses = together(makers)
    done = inverted(done)
    firsts, seconds, tops, wholes = [], [], [], []
    for h in heads:
        right = rights[h]
        inv = jnp.where(lane < half, inverses[h], 0.0)
        firsts.append(right[:half] + dot_once(inv, right[:top], ROWS))
    for h in heads:
        across = jnp.where(lane < half, lower_top[h][half:], 0.0)
        seconds.append(
            rights[h][half:top]
            - dot_once(across, jnp.concatenate([firsts[h]] * 2, axis=0), ROWS)
        )
    for h in heads:
        inv = jnp.where(lane >= half, inverses[h], 0.0)
        tops.append(
            jnp.concatenate(
                [
                    firsts[h],
                    seconds[h] + dot_once(inv, jnp.concatenate([seconds[h]] * 2, axis=0), ROWS),
                ],
                axis=0,
            ).astype(jnp.bfloat16)
        )
    thirds = [
        rights[h][top:] - dot_once(lower_bot[h][:, :top], tops[h], ROWS) for h in heads
    ]
    for h in heads:
        inv = inverses[per_group + h // 2]
        inv = jnp.where(lane < half, inv, 0.0) if h % 2 == 0 else jnp.where(lane >= half, inv, 0.0)
        third = thirds[h] + dot_once(inv, jnp.concatenate([thirds[h]] * 2, axis=0), ROWS)
        wholes.append(jnp.concatenate([tops[h], third.astype(jnp.bfloat16)], axis=0))
    eye = iota2((state_dim, state_dim), 0) == iota2((state_dim, state_dim), 1)
    for h in heads:
        moved = dot_once(key_decay[h], wholes[h], OVER)
        head = g * per_group + h
        transition_ref[head] = (
            jnp.where(eye, kept[h], 0.0) - moved[:, :state_dim]
        ).astype(transition_ref.dtype)
        offset_ref[head] = moved[:, state_dim:]
    for h in heads:
        read = dot_once(attend_top[h], tops[h], ROWS)
        readout_ref[:top, at[h]] = (read_query[h][:top] - read[:, :state_dim]).astype(
            readout_ref.dtype
        )
        local_ref[:top, at[h]] = read[:, state_dim:]
        read = dot_once(attend_bot[h][:, :tokens], wholes[h], ROWS)
        readout_ref[top:, at[h]] = (read_query[h][top:] - read[:, :state_dim]).astype(
            readout_ref.dtype
        )
        local_ref[top:, at[h]] = read[:, state_dim:]
    return done


def attend_step(
    half, step, group, query_ref, even_ref, odd_ref, bias_ref, up_ref, out_ref,
    *, width, first_key, key_count, score_scale,
):
    rows = out_ref.shape[0]
    wide = even_ref.shape[1]
    lat_dim, vhead = up_ref.shape[1:]
    pairs = group // 2
    keys = pl.ds(pl.multiple_of(half * rows + first_key, math.gcd(rows, first_key)), key_count)
    own = pl.ds(pl.multiple_of(half * rows, rows), rows)
    bias = bias_ref[half]
    contexts = []
    for key_ref, skip in ((even_ref, 0), (odd_ref, 2 * width - wide)):
        stacked = []
        for p in range(pairs):
            begin = (step * group + 2 * p) * width + skip
            stacked.append(query_ref[own, pl.ds(pl.multiple_of(begin, 128), wide)])
        query = jnp.concatenate(stacked, axis=0) if pairs > 1 else stacked[0]
        scores = lax.dot_general(
            query, key_ref[keys, :], TRANS, preferred_element_type=jnp.float32
        )
        scores = scores.reshape(pairs, rows, key_count) * score_scale + bias[None]
        exponent = jnp.exp(scores - jnp.max(scores, axis=2, keepdims=True))
        exponent = exponent.reshape(pairs * rows, key_count)
        row_total = jnp.sum(exponent, axis=1, keepdims=True)
        weighted = jnp.dot(
            exponent.astype(jnp.bfloat16),
            even_ref[keys, :lat_dim],
            preferred_element_type=jnp.float32,
        )
        contexts.append((weighted / row_total).astype(jnp.bfloat16))
    for p in range(pairs):
        for parity in range(2):
            head = step * group + 2 * p + parity
            out_ref[:, pl.ds(pl.multiple_of(head * vhead, vhead), vhead)] = jnp.dot(
                contexts[parity][p * rows : (p + 1) * rows],
                up_ref[head],
                preferred_element_type=jnp.float32,
            ).astype(jnp.bfloat16)


def layers(
    lengths_hbm, kq_hbm, kk_hbm, kv_hbm, kg_hbm, strength_hbm, mq_hbm, lat_hbm, up_hbm, proj_hbm,
    kda_stage, mixed_stage,
    lengths_ref, kq, kk, kv, kg, strength, mq, window, even, odd, up, proj,
    rel_top, rel_bot, carried, tail, beta, readout, local_part, transition, offset,
    state_out, state_in, bias, head_out, far_send, far_recv, near_part,
    kda_sem, load_sem, lat_send, lat_recv, pass_send, pass_recv,
    state_send, state_recv, far_ssem, far_rsem,
    *, hops, need, width, per_group, per_step, per_pass, first_key, key_count, score_scale, exchange,
):
    tokens, lanes = kq.shape
    heads = strength.shape[0]
    state_dim = lanes // heads
    groups = heads // per_group
    steps = heads // per_step
    passes = heads // per_pass
    rows = tokens // 2
    ctx_count = lax.axis_size("ctx")
    place = lax.axis_index("ctx")
    mine = lax.axis_index("head")
    model = proj.shape[1]
    pieces = model // CHUNK
    first = place * tokens

    def up_by(by):
        return {"ctx": place + by}

    partner = {"head": 1 - mine}

    def load(source, target, sem):
        return pltpu.make_async_copy(source, target, sem)

    def kda_loads(g):
        part = pl.ds(pl.multiple_of(g * per_group * state_dim, state_dim), per_group * state_dim)
        return [
            load(source.at[0, :, part], target.at[:, part], kda_sem.at[g, n])
            for n, (source, target) in enumerate(
                ((kg_hbm, kg), (kq_hbm, kq), (kk_hbm, kk), (kv_hbm, kv))
            )
        ]

    strength_copy = load(strength_hbm.at[0], strength, load_sem.at[0])
    lat_copy = load(lat_hbm.at[0], window, load_sem.at[1])
    mq_copy = load(mq_hbm.at[0], mq, load_sem.at[2])
    up_copy = load(up_hbm, up, load_sem.at[3])
    proj_copy = load(proj_hbm, proj, load_sem.at[4])
    lengths_copy = load(lengths_hbm, lengths_ref, load_sem.at[5])

    barrier = pltpu.get_barrier_semaphore()
    halved = exchange and hops == 2 and need == [tokens, rows]
    peers = jnp.int32(0)
    for by in range(1, 2 if halved else hops + 1):
        for sign in (1, -1):
            there = place + sign * by
            known = (there >= 0) & (there < ctx_count)
            peers = peers + jnp.where(known, 1, 0)

            @pl.when(known)
            def _():
                pl.semaphore_signal(
                    barrier, inc=1, device_id={"ctx": there}, device_id_type=MESH
                )

    if exchange:
        pl.semaphore_signal(barrier, inc=1, device_id=partner, device_id_type=MESH)
        peers = peers + 1

    lat_copy.start()
    lengths_copy.start()
    strength_copy.start()
    for g in range(groups):
        for copy in kda_loads(g):
            copy.start()


    def lat_copy_to(by):
        count = rows if halved else need[by - 1]
        begin = pl.multiple_of(rows * mine, rows) if halved else tokens - count
        behind = by - 1 if halved else 0
        return pltpu.make_async_remote_copy(
            src_ref=even.at[pl.ds(begin + (hops - behind) * tokens, count)],
            dst_ref=even.at[pl.ds(begin + (hops - by) * tokens, count)],
            send_sem=lat_send.at[by - 1],
            recv_sem=lat_recv.at[by - 1],
            device_id=up_by(1 if halved else by),
            device_id_type=MESH,
        )

    def lat_pass(by):
        begin = pl.multiple_of(rows * mine, rows)
        region = even.at[pl.ds(begin + (hops - by) * tokens, rows)]
        return pltpu.make_async_remote_copy(
            src_ref=region,
            dst_ref=even.at[pl.ds(begin + (hops - by) * tokens, rows)],
            send_sem=pass_send.at[by - 1],
            recv_sem=pass_recv.at[by - 1],
            device_id=partner,
            device_id_type=MESH,
        )

    direct = range(1, 2 if halved else hops + 1)
    upper = mine == 1
    sends_on = upper & (place >= 1) & (place + 1 < ctx_count)
    far_comes = place >= 2

    blank = jnp.zeros((tokens, even.shape[1] - width), even.dtype)
    lat_copy.wait()
    even[hops * tokens :] = jnp.concatenate([window[...], blank], axis=1)
    pl.semaphore_wait(barrier, peers)
    for by in direct:

        @pl.when(place + by < ctx_count)
        def _():
            lat_copy_to(by).start()

    mq_copy.start()
    up_copy.start()
    proj_copy.start()

    def state_copy(c):
        part = pl.ds(c * per_pass, per_pass)
        return pltpu.make_async_remote_copy(
            src_ref=state_out.at[part],
            dst_ref=state_in.at[part],
            send_sem=state_send.at[c],
            recv_sem=state_recv.at[c],
            device_id=up_by(1),
            device_id_type=MESH,
        )

    def relay(c, _):
        @pl.when(place > 0)
        def _():
            state_copy(c).wait_recv()

        @pl.when(place == 0)
        def _():
            for n in range(per_pass):
                head = c * per_pass + n
                state_out[head] = offset[head].astype(state_out.dtype)

        @pl.when((place > 0) & (place + 1 < ctx_count))
        def _():
            for n in range(per_pass):
                head = c * per_pass + n
                state_out[head] = (
                    offset[head]
                    + jnp.dot(
                        transition[head], state_in[head], preferred_element_type=jnp.float32
                    )
                ).astype(state_out.dtype)

        @pl.when(place + 1 < ctx_count)
        def _():
            state_copy(c).start()

        return 0

    passes_group = passes // groups

    def relay_slot(time, ready, before):
        due = (time - FIRST_PASS - HOP_LATE * (place - 1)) // PASS_TIME + 1
        due = jnp.where(place == 0, ready, jnp.where(place == ctx_count - 1, 0, due))
        after = jnp.maximum(before, jnp.minimum(due, passes))
        lax.fori_loop(before, after, relay, 0)
        return after

    for by in range(1, hops + 1):

        @pl.when(place < by)
        def _():
            stop = (hops - by + 1) * tokens
            even[stop - need[by - 1] : stop] = jnp.zeros(
                (need[by - 1], even.shape[1]), even.dtype
            )

    lengths_copy.wait()
    strength_copy.wait()
    delta_setup(
        lengths_ref, strength, rel_top, rel_bot, carried, tail, beta, first, per_group
    )
    pos_q = first + iota2((tokens, 1), 0)
    for n in range(2):
        q = slice(n * rows, (n + 1) * rows)
        pos_key = pos_q[n * rows : n * rows + 1] - (key_count - rows) + iota2((1, key_count), 1)
        doc_q, doc_key = jnp.zeros((rows, 1), jnp.int32), jnp.zeros_like(pos_key)
        end = jnp.int32(0)
        for d in range(lengths_ref.shape[1]):
            end = end + lengths_ref[0, d]
            doc_q = doc_q + jnp.where(pos_q[q] >= end, 1, 0)
            doc_key = doc_key + jnp.where(pos_key >= end, 1, 0)
        bias[n] = jnp.where(
            (pos_key <= pos_q[q]) & (pos_key >= 0) & (doc_key == doc_q), 0.0, masked_score
        )

    def pass_latents():
        @pl.when(place >= 1)
        def _():
            lat_copy_to(1).wait_recv()

        @pl.when(sends_on)
        def _():
            lat_copy_to(2).start()

        @pl.when(place >= 1)
        def _():
            lat_pass(1).start()

    def delta_step(g, done):
        for copy in kda_loads(g):
            copy.wait()
        begin = DELTA_AT + DELTA_TIME * g // groups

        def scored(done):
            return relay_slot(begin + DELTA_TIME * 2 // (5 * groups), passes_group * g, done)

        def inverted(done):
            return relay_slot(begin + DELTA_TIME * 3 // (4 * groups), passes_group * g, done)

        done = delta_group(
            g, per_group, kq, kk, kv, kg, beta, rel_top, rel_bot, carried, tail,
            readout, local_part, transition, offset, scored, inverted, done,
        )
        done = relay_slot(begin + DELTA_TIME // groups, passes_group * (g + 1), done)
        if halved:
            pl.when(g == 0)(pass_latents)

        return done

    done = lax.fori_loop(0, groups, delta_step, jnp.int32(0))

    def shifted(n):
        begin = first_key if n == 0 else 0
        part = slice(n * tokens + begin, (n + 1) * tokens)
        odd[part] = jnp.concatenate([blank[begin:], even[part][:, :width]], axis=1)

    if halved:

        @pl.when(place >= 1)
        def _():
            lat_pass(1).wait_recv()

        @pl.when(upper & far_comes)
        def _():
            lat_copy_to(2).wait_recv()
            lat_pass(2).start()

        @pl.when(upper)
        def _():
            shifted(0)

    else:
        for by in direct:

            @pl.when(place >= by)
            def _():
                lat_copy_to(by).wait_recv()

            shifted(hops - by)

    def last_latents():
        @pl.when(far_comes)
        def _():
            lat_pass(2).wait_recv()

        shifted(0)

    for n in range(1 if halved else hops, hops + 1):
        shifted(n)

    def far_copy(n):
        return pltpu.make_async_remote_copy(
            src_ref=far_send.at[n],
            dst_ref=far_recv.at[n],
            send_sem=far_ssem.at[n],
            recv_sem=far_rsem.at[n],
            device_id=partner,
            device_id_type=MESH,
        )

    far_half = 1 - mine if exchange else 0
    near_half = mine if exchange else 1
    up_copy.wait()
    mq_copy.wait()

    def attention(turn, done):
        half = jnp.where(turn == 0, far_half, near_half)
        if halved:
            pl.when((turn == 1) & (mine == 0))(last_latents)
        time = TURN_AT + turn * (ATTEND_TIME + PROJECT_TIME)

        def attend_turn(step, done):
            attend_step(
                half, step, per_step, mq, even, odd, bias, up, head_out,
                width=width, first_key=first_key, key_count=key_count, score_scale=score_scale,
            )
            return relay_slot(time + ATTEND_TIME * (step + 1) // steps, passes, done)

        done = lax.fori_loop(0, steps, attend_turn, done)

        @pl.when(turn == 0)
        def _():
            proj_copy.wait()

        def project(n, done):
            part = jnp.dot(
                head_out[...],
                proj[:, pl.ds(pl.multiple_of(n * CHUNK, CHUNK), CHUNK)],
                preferred_element_type=jnp.float32,
            )

            @pl.when(turn == 0)
            def _():
                far_send[n] = part.astype(jnp.bfloat16)
                if exchange:
                    far_copy(n).start()

            @pl.when(turn == 1)
            def _():
                near_part[n] = part

            return relay_slot(
                time + ATTEND_TIME + PROJECT_TIME * (n + 1) // pieces, passes, done
            )

        return lax.fori_loop(0, pieces, project, done)

    done = lax.fori_loop(0, 2, attention, done)

    def read_heads(c, _):
        @pl.when(c >= done)
        def _():
            relay(c, 0)

        for n in range(per_pass):
            head = c * per_pass + n
            at = pl.ds(pl.multiple_of(head * state_dim, state_dim), state_dim)

            @pl.when(place > 0)
            def _():
                kda_stage[0, :, at] = (
                    local_part[:, at]
                    + jnp.dot(readout[:, at], state_in[head], preferred_element_type=jnp.float32)
                ).astype(kda_stage.dtype)

            @pl.when(place == 0)
            def _():
                kda_stage[0, :, at] = local_part[:, at].astype(kda_stage.dtype)

        return 0

    lax.fori_loop(0, passes, read_heads, 0)

    def mix(n, _):
        at = pl.ds(pl.multiple_of(n * CHUNK, CHUNK), CHUNK)
        if exchange:
            far_copy(n).wait_recv()
            mixed_stage[0, :, at] = (near_part[n] + far_recv[n].astype(jnp.float32)).astype(
                jnp.bfloat16
            )
        else:
            mixed_stage[0, :rows, at] = far_send[n]
            mixed_stage[0, rows:, at] = near_part[n].astype(jnp.bfloat16)
        return 0

    lax.fori_loop(0, pieces, mix, 0)

    for by in direct:

        @pl.when(place + by < ctx_count)
        def _():
            lat_copy_to(by).wait_send()

    if halved:

        @pl.when(place >= 1)
        def _():
            lat_pass(1).wait_send()

        @pl.when(sends_on)
        def _():
            lat_copy_to(2).wait_send()

        @pl.when(upper & far_comes)
        def _():
            lat_pass(2).wait_send()

    @pl.when(place + 1 < ctx_count)
    def _():
        for c in range(passes):
            state_copy(c).wait_send()

    if exchange:
        for n in range(pieces):
            far_copy(n).wait_send()


def write_out(kda_ref, mixed_ref, kda_hbm, mixed_hbm, sem):
    copies = [
        pltpu.make_async_copy(kda_ref, kda_hbm, sem.at[0]),
        pltpu.make_async_copy(mixed_ref, mixed_hbm, sem.at[1]),
    ]
    for copy in copies:
        copy.start()
    for copy in copies:
        copy.wait()


def local(
    kda_query, kda_key, kda_value, log_decay, write_strength, mla_query, latents, value_up,
    out_proj, doc_lengths,
):
    tokens = kda_query.shape[1]
    heads = write_strength.shape[1]
    lanes = kda_query.shape[2]
    state_dim = lanes // heads
    ctx_count = lax.axis_size("ctx")
    head_count = lax.axis_size("head")
    exchange = head_count == 2
    longest = 3 * tokens * ctx_count // 8
    hops = min(ctx_count - 1, -(-(longest - 1) // tokens))
    width = latents.shape[2]
    spare = -width % 128
    model = out_proj.shape[1]
    rows = tokens // 2
    back = -(-(longest - 1) // rows) * rows
    first_key = hops * tokens - back
    need = [min(tokens, back - (by - 1) * tokens) for by in range(1, hops + 1)]
    per_group = math.gcd(heads, 8)
    per_step = math.gcd(heads, 8)
    per_pass = 2
    top = 2 * (tokens // 3)
    wide = 2 * top
    groups, steps, passes, pieces = (
        heads // per_group, heads // per_step, heads // per_pass, model // CHUNK,
    )
    window_rows = (hops + 1) * tokens
    bf16, f32 = jnp.bfloat16, jnp.float32
    vmem = pltpu.VMEM
    dma = pltpu.SemaphoreType.DMA
    scratch = [
        pltpu.SMEM(doc_lengths.shape, jnp.int32),
        vmem((tokens, lanes), bf16),
        vmem((tokens, lanes), bf16),
        vmem((tokens, lanes), bf16),
        vmem((tokens, lanes), bf16),
        vmem((heads, tokens), f32),
        vmem((tokens, heads * width), bf16),
        vmem((tokens, width), bf16),
        vmem((window_rows, width + spare), bf16),
        vmem((window_rows, width + spare), bf16),
        vmem(value_up.shape, bf16),
        vmem(out_proj.shape, bf16),
        vmem((top, top), jnp.int32),
        vmem((tokens - top, wide), jnp.int32),
        vmem((tokens, state_dim), f32),
        vmem((tokens, state_dim), f32),
        vmem((groups, tokens, 128), f32),
        vmem((tokens, lanes), bf16),
        vmem((tokens, lanes), f32),
        vmem((heads, state_dim, state_dim), bf16),
        vmem((heads, state_dim, state_dim), f32),
        vmem((heads, state_dim, state_dim), bf16),
        vmem((heads, state_dim, state_dim), bf16),
        vmem((2, rows, back + rows), f32),
        vmem((rows, heads * value_up.shape[2]), bf16),
        vmem((pieces, rows, CHUNK), bf16),
        vmem((pieces, rows, CHUNK), bf16),
        vmem((pieces, rows, CHUNK), f32),
        dma((groups, 4)),
        dma((6,)),
        dma((hops,)),
        dma((hops,)),
        dma((hops,)),
        dma((hops,)),
        dma((passes,)),
        dma((passes,)),
        dma((pieces,)),
        dma((pieces,)),
    ]
    anywhere = pl.BlockSpec(memory_space=pl.ANY)
    kda_out, mixed = pl.pallas_call(
        functools.partial(
            layers, hops=hops, need=need, width=width, per_group=per_group, per_step=per_step,
            per_pass=per_pass, first_key=first_key, key_count=back + rows,
            score_scale=1.0 / math.sqrt(NOPE + ROPE), exchange=exchange,
        ),
        in_specs=[anywhere] * 10,
        out_specs=[pl.BlockSpec(memory_space=pltpu.VMEM)] * 2,
        out_shape=[
            pltpu.VMEM((1, tokens, lanes), bf16),
            pltpu.VMEM((1, rows if exchange else tokens, model), bf16),
        ],
        scratch_shapes=scratch,
        compiler_params=pltpu.CompilerParams(
            vmem_limit_bytes=58 << 20, collective_id=0, has_side_effects=True
        ),
        cost_estimate=pl.CostEstimate(
            flops=10_000_000_000, bytes_accessed=20_000_000, transcendentals=0
        ),
    )(
        in_place(doc_lengths), in_place(kda_query), in_place(kda_key), in_place(kda_value),
        in_place(log_decay), in_place(write_strength), in_place(mla_query), in_place(latents),
        in_place(value_up), in_place(out_proj),
    )
    if not exchange:
        mixed = lax.psum_scatter(mixed, "head", scatter_dimension=1, tiled=True)
        return kda_out, mixed
    return pl.pallas_call(
        write_out,
        in_specs=[pl.BlockSpec(memory_space=pltpu.VMEM)] * 2,
        out_specs=[anywhere] * 2,
        out_shape=[pltpu.HBM(kda_out.shape, bf16), pltpu.HBM(mixed.shape, bf16)],
        scratch_shapes=[dma((2,))],
        compiler_params=pltpu.CompilerParams(vmem_limit_bytes=4 << 20),
    )(
        pltpu.with_memory_space_constraint(kda_out, pltpu.VMEM),
        pltpu.with_memory_space_constraint(mixed, pltpu.VMEM),
    )


def solution(mesh):
    placed = (
        P(("group", "req"), "ctx", "head"),
        P(("group", "req"), "ctx", "head"),
        P(("group", "req"), "ctx", "head"),
        P(("group", "req"), "ctx", "head"),
        P(("group", "req"), "head", "ctx"),
        P(("group", "req"), "ctx", "head"),
        P(("group", "req"), "ctx", None),
        P("head", None, None),
        P("head", None),
        P(("group", "req"), None),
    )
    return jax.shard_map(
        local,
        mesh=mesh,
        in_specs=placed,
        out_specs=(P(("group", "req"), "ctx", "head"), P(("group", "req"), ("ctx", "head"), None)),
        check_vma=False,
    )
```

```python
import functools
import math

import jax
import jax.numpy as jnp
from jax import lax
from jax.experimental import pallas as pl
from jax.experimental.pallas import tpu as pltpu
from jax.sharding import PartitionSpec as P

ROPE = 64
NOPE = 128
MESH = pl.DeviceIdType.MESH
CHUNK = 256

DELTA_AT = 26
DELTA_TIME = 78
TURN_AT = 107
ATTEND_TIME = 35
PROJECT_TIME = 28
FIRST_PASS = 87
HOP_LATE = 39
PASS_TIME = 14

masked_score = -1e30
ROWS = (((1,), (0,)), ((), ()))
TRANS = (((1,), (1,)), ((), ()))
OVER = (((0,), (0,)), ((), ()))


def in_place(value):
    return pltpu.with_memory_space_constraint(value, pltpu.HBM)


def dot_once(left, right, dims):
    return lax.dot_general(
        left.astype(jnp.bfloat16),
        right.astype(jnp.bfloat16),
        dims,
        preferred_element_type=jnp.float32,
    )


def iota2(shape, axis):
    return lax.broadcasted_iota(jnp.int32, shape, axis)


def delta_setup(lengths_ref, strength_ref, rel_top, rel_bot, carried_ref, tail_ref, beta_ref, first, per_group):
    tokens, state_dim = carried_ref.shape
    top = rel_top.shape[0]
    wide = rel_bot.shape[1]
    bot = tokens - top
    pos_col = first + iota2((tokens, 1), 0)
    pos_row = first + iota2((1, wide), 1)
    doc_col, doc_row = jnp.zeros_like(pos_col), jnp.zeros_like(pos_row)
    prev_doc, last_doc, end = jnp.int32(0), jnp.int32(0), jnp.int32(0)
    for d in range(lengths_ref.shape[1]):
        end = end + lengths_ref[0, d]
        doc_col = doc_col + jnp.where(pos_col >= end, 1, 0)
        doc_row = doc_row + jnp.where(pos_row >= end, 1, 0)
        prev_doc = prev_doc + jnp.where(first - 1 >= end, 1, 0)
        last_doc = last_doc + jnp.where(first + tokens - 1 >= end, 1, 0)
    rel_top[...] = jnp.where(
        doc_col[:top] == doc_row[:, :top], iota2((top, top), 0) - iota2((top, top), 1), -1
    )
    rel_bot[...] = jnp.where(
        (doc_col[top:] == doc_row) & (iota2((bot, wide), 1) < tokens),
        iota2((bot, wide), 0) + top - iota2((bot, wide), 1),
        -1,
    )
    ones = jnp.ones((1, state_dim), jnp.float32)
    carried_ref[...] = jnp.where(doc_col == prev_doc, 1.0, 0.0) * ones
    tail_ref[...] = jnp.where(doc_col == last_doc, 1.0, 0.0) * ones
    heads = strength_ref.shape[0]
    padded = jnp.concatenate(
        [strength_ref[...], jnp.zeros((heads, wide - tokens), jnp.float32)], axis=1
    )
    padded = jnp.concatenate([padded, jnp.zeros((128 - heads, wide), jnp.float32)], axis=0)
    turned = jnp.transpose(padded)[:tokens]
    for g in range(heads // per_group):
        beta_ref[g] = turned if g == 0 else pltpu.roll(turned, 128 - g * per_group, 1)


def packed_inverse(pack):
    lane = iota2((1, 128), 1)
    piece = pack[0:16]
    for b in range(1, 4):
        piece = jnp.where((lane % 64) // 16 == b, pack[16 * b : 16 * b + 16], piece)
    row16, col16 = iota2((16, 128), 0), iota2((16, 128), 1) % 16
    inv = jnp.where((row16 // 2 == col16 // 2) & (row16 > col16), -piece, 0.0)
    yield
    for width, size in ((2, 16), (4, 16), (8, 16), (16, 32), (32, 64)):
        if size == 32:
            piece = jnp.where((lane % 64) // 32 == 0, pack[0:32], pack[32:64])
        elif size == 64:
            piece = pack
        if width == size // 2 and size > 16:
            inv = jnp.concatenate(
                [
                    jnp.where(lane % size < width, inv, 0.0),
                    jnp.where(lane % size >= width, inv, 0.0),
                ],
                axis=0,
            )
        row, col = iota2((size, 128), 0), iota2((size, 128), 1) % size
        corner = (row // (2 * width) == col // (2 * width)) & (row // width > col // width)
        part = jnp.where(corner, piece, 0.0)
        left = part + dot_once(inv, spread(part, size), ROWS)
        yield
        inv = inv - (left + dot_once(left, spread(inv, size), ROWS))
        yield
    yield inv


def spread(cells, size):
    copies = 128 // size
    own = iota2((128, 128), 0) // size == iota2((128, 128), 1) // size
    return jnp.where(own, jnp.concatenate([cells] * copies, axis=0), 0.0).astype(jnp.bfloat16)


def together(makers):
    done = []
    while True:
        step = [next(m) for m in makers]
        if step[0] is not None:
            return step


def delta_group(
    g, per_group, query_ref, key_ref, value_ref, decay_ref, beta_ref, rel_top, rel_bot,
    carried_ref, tail_ref, readout_ref, local_ref, transition_ref, offset_ref,
    scored, inverted, stated, done,
):
    tokens, state_dim = carried_ref.shape
    top = rel_top.shape[0]
    half = top // 2
    heads = range(per_group)
    inclusive = jnp.where(
        iota2((tokens, tokens), 0) >= iota2((tokens, tokens), 1), 1.0, 0.0
    ).astype(jnp.bfloat16)
    lane = iota2((1, 128), 1)
    at = [
        pl.ds(pl.multiple_of((g * per_group + h) * state_dim, state_dim), state_dim) for h in heads
    ]
    summed = []
    for h in range(0, per_group, 2):
        both = pl.ds(
            pl.multiple_of((g * per_group + h) * state_dim, 2 * state_dim), 2 * state_dim
        )
        pair = jnp.dot(inclusive, decay_ref[:, both], preferred_element_type=jnp.float32)
        summed += [pair[:, :state_dim], pair[:, state_dim:]]
    lower_top, lower_bot, attend_top, attend_bot = [], [], [], []
    right_keys, read_query, key_decay, kept, rights = [], [], [], [], []
    for h in heads:
        s = summed[h]
        query = query_ref[:, at[h]].astype(jnp.float32)
        key = key_ref[:, at[h]].astype(jnp.float32)
        beta = beta_ref[g, :, h : h + 1]
        query = query * lax.rsqrt(jnp.sum(query * query, axis=1, keepdims=True) + 1e-06)
        key = key * lax.rsqrt(jnp.sum(key * key, axis=1, keepdims=True) + 1e-06)
        written = key * beta
        mid, start, last = s[half - 1 : half], s[top - 1 : top], s[tokens - 1 : tokens]
        fall_top, fall_bot = jnp.exp(s[:top] - mid), jnp.exp(s[top:] - start)
        lift_top, lift_bot = jnp.exp(mid - s[:top]), jnp.exp(start - s[top:])
        to_mid, to_start, mid_start = jnp.exp(mid), jnp.exp(start), jnp.exp(start - mid)
        key_top, key_bot = written[:top] * fall_top, written[top:] * fall_bot
        query_top, query_bot = query[:top] * fall_top, query[top:] * fall_bot
        raised_top = key[:top] * lift_top
        raised_all = jnp.concatenate([raised_top * mid_start, key[top:] * lift_bot], axis=0)
        both_top = dot_once(
            jnp.concatenate([key_top, query_top], axis=0), raised_top, TRANS
        )
        both_bot = dot_once(
            jnp.concatenate([key_bot, query_bot], axis=0),
            jnp.concatenate([raised_all, jnp.zeros((half, state_dim), jnp.float32)], axis=0),
            TRANS,
        )
        lower_top.append(jnp.where(rel_top[...] > 0, both_top[:top], 0.0))
        attend_top.append(jnp.where(rel_top[...] >= 0, both_top[top:], 0.0).astype(jnp.bfloat16))
        lower_bot.append(jnp.where(rel_bot[...] > 0, both_bot[:half], 0.0))
        attend_bot.append(
            jnp.where(rel_bot[...] >= 0, both_bot[half:], 0.0).astype(jnp.bfloat16)
        )
        carried = carried_ref[...]
        grown = jnp.concatenate([key_top * to_mid, key_bot * to_start], axis=0) * carried
        read_query.append(
            jnp.concatenate([query_top * to_mid, query_bot * to_start], axis=0) * carried
        )
        key_decay.append((raised_all * jnp.exp(last - start) * tail_ref[...]).astype(jnp.bfloat16))
        kept.append(jnp.exp(last) * carried[tokens - 1 : tokens])
        rights.append(
            jnp.concatenate([grown, value_ref[:, at[h]].astype(jnp.float32) * beta], axis=1)
        )
    done = scored(done)
    makers = [
        packed_inverse(jnp.where(lane < half, lower_top[h][:half], lower_top[h][half:]))
        for h in heads
    ]
    makers += [
        packed_inverse(
            jnp.where(
                lane < half,
                lower_bot[h][:, top:],
                pltpu.roll(lower_bot[h + 1][:, top:], half, 1),
            )
        )
        for h in range(0, per_group, 2)
    ]
    inverses = together(makers)
    done = inverted(done)
    firsts, seconds, tops, wholes = [], [], [], []
    for h in heads:
        right = rights[h]
        inv = jnp.where(lane < half, inverses[h], 0.0)
        firsts.append(right[:half] + dot_once(inv, right[:top], ROWS))
    for h in heads:
        across = jnp.where(lane < half, lower_top[h][half:], 0.0)
        seconds.append(
            rights[h][half:top]
            - dot_once(across, jnp.concatenate([firsts[h]] * 2, axis=0), ROWS)
        )
    for h in heads:
        inv = jnp.where(lane >= half, inverses[h], 0.0)
        tops.append(
            jnp.concatenate(
                [
                    firsts[h],
                    seconds[h] + dot_once(inv, jnp.concatenate([seconds[h]] * 2, axis=0), ROWS),
                ],
                axis=0,
            ).astype(jnp.bfloat16)
        )
    thirds = [
        rights[h][top:] - dot_once(lower_bot[h][:, :top], tops[h], ROWS) for h in heads
    ]
    for h in heads:
        inv = inverses[per_group + h // 2]
        inv = jnp.where(lane < half, inv, 0.0) if h % 2 == 0 else jnp.where(lane >= half, inv, 0.0)
        third = thirds[h] + dot_once(inv, jnp.concatenate([thirds[h]] * 2, axis=0), ROWS)
        wholes.append(jnp.concatenate([tops[h], third.astype(jnp.bfloat16)], axis=0))
    eye = iota2((state_dim, state_dim), 0) == iota2((state_dim, state_dim), 1)
    for h in heads:
        moved = dot_once(key_decay[h], wholes[h], OVER)
        head = g * per_group + h
        transition_ref[head] = (
            jnp.where(eye, kept[h], 0.0) - moved[:, :state_dim]
        ).astype(transition_ref.dtype)
        offset_ref[head] = moved[:, state_dim:]
    done = stated(done)
    for h in heads:
        read = dot_once(attend_top[h], tops[h], ROWS)
        readout_ref[:top, at[h]] = (read_query[h][:top] - read[:, :state_dim]).astype(
            readout_ref.dtype
        )
        local_ref[:top, at[h]] = read[:, state_dim:]
        read = dot_once(attend_bot[h][:, :tokens], wholes[h], ROWS)
        readout_ref[top:, at[h]] = (read_query[h][top:] - read[:, :state_dim]).astype(
            readout_ref.dtype
        )
        local_ref[top:, at[h]] = read[:, state_dim:]
    return done


def attend_step(
    half, step, group, query_ref, even_ref, odd_ref, bias_ref, up_ref, out_ref,
    *, width, first_key, key_count, score_scale,
):
    rows = out_ref.shape[0]
    wide = even_ref.shape[1]
    lat_dim, vhead = up_ref.shape[1:]
    pairs = group // 2
    keys = pl.ds(pl.multiple_of(half * rows + first_key, math.gcd(rows, first_key)), key_count)
    own = pl.ds(pl.multiple_of(half * rows, rows), rows)
    bias = bias_ref[half]
    contexts = []
    for key_ref, skip in ((even_ref, 0), (odd_ref, 2 * width - wide)):
        stacked = []
        for p in range(pairs):
            begin = (step * group + 2 * p) * width + skip
            stacked.append(query_ref[own, pl.ds(pl.multiple_of(begin, 128), wide)])
        query = jnp.concatenate(stacked, axis=0) if pairs > 1 else stacked[0]
        scores = lax.dot_general(
            query, key_ref[keys, :], TRANS, preferred_element_type=jnp.float32
        )
        scores = scores.reshape(pairs, rows, key_count) * score_scale + bias[None]
        exponent = jnp.exp(scores - jnp.max(scores, axis=2, keepdims=True))
        exponent = exponent.reshape(pairs * rows, key_count)
        row_total = jnp.sum(exponent, axis=1, keepdims=True)
        weighted = jnp.dot(
            exponent.astype(jnp.bfloat16),
            even_ref[keys, :lat_dim],
            preferred_element_type=jnp.float32,
        )
        contexts.append((weighted / row_total).astype(jnp.bfloat16))
    for p in range(pairs):
        for parity in range(2):
            head = step * group + 2 * p + parity
            out_ref[:, pl.ds(pl.multiple_of(head * vhead, vhead), vhead)] = jnp.dot(
                contexts[parity][p * rows : (p + 1) * rows],
                up_ref[head],
                preferred_element_type=jnp.float32,
            ).astype(jnp.bfloat16)


def layers(
    lengths_hbm, kq_hbm, kk_hbm, kv_hbm, kg_hbm, strength_hbm, mq_hbm, lat_hbm, up_hbm, proj_hbm,
    kda_stage, mixed_stage,
    lengths_ref, kq, kk, kv, kg, strength, mq, window, even, odd, up, proj,
    rel_top, rel_bot, carried, tail, beta, readout, local_part, transition, offset,
    state_out, state_in, bias, head_out, far_send, far_recv, near_part,
    kda_sem, load_sem, lat_send, lat_recv, pass_send, pass_recv,
    state_send, state_recv, far_ssem, far_rsem,
    *, hops, need, width, per_group, per_step, per_pass, first_key, key_count, score_scale, exchange,
):
    tokens, lanes = kq.shape
    heads = strength.shape[0]
    state_dim = lanes // heads
    groups = heads // per_group
    steps = heads // per_step
    passes = heads // per_pass
    rows = tokens // 2
    ctx_count = lax.axis_size("ctx")
    place = lax.axis_index("ctx")
    mine = lax.axis_index("head")
    model = proj.shape[1]
    pieces = model // CHUNK
    joined = math.gcd(pieces, 3)
    first = place * tokens

    def up_by(by):
        return {"ctx": place + by}

    partner = {"head": 1 - mine}

    def load(source, target, sem):
        return pltpu.make_async_copy(source, target, sem)

    def kda_loads(g):
        part = pl.ds(pl.multiple_of(g * per_group * state_dim, state_dim), per_group * state_dim)
        return [
            load(source.at[0, :, part], target.at[:, part], kda_sem.at[g, n])
            for n, (source, target) in enumerate(
                ((kg_hbm, kg), (kq_hbm, kq), (kk_hbm, kk), (kv_hbm, kv))
            )
        ]

    strength_copy = load(strength_hbm.at[0], strength, load_sem.at[0])
    lat_copy = load(lat_hbm.at[0], window, load_sem.at[1])
    mq_copy = load(mq_hbm.at[0], mq, load_sem.at[2])
    up_copy = load(up_hbm, up, load_sem.at[3])
    proj_copy = load(proj_hbm, proj, load_sem.at[4])
    lengths_copy = load(lengths_hbm, lengths_ref, load_sem.at[5])

    barrier = pltpu.get_barrier_semaphore()
    halved = exchange and hops == 2 and need == [tokens, rows]
    peers = jnp.int32(0)
    for by in range(1, 2 if halved else hops + 1):
        for sign in (1, -1):
            there = place + sign * by
            known = (there >= 0) & (there < ctx_count)
            peers = peers + jnp.where(known, 1, 0)

            @pl.when(known)
            def _():
                pl.semaphore_signal(
                    barrier, inc=1, device_id={"ctx": there}, device_id_type=MESH
                )

    if exchange:
        pl.semaphore_signal(barrier, inc=1, device_id=partner, device_id_type=MESH)
        peers = peers + 1

    lat_copy.start()
    lengths_copy.start()
    strength_copy.start()
    for g in range(groups):
        for copy in kda_loads(g):
            copy.start()


    def lat_copy_to(by):
        count = rows if halved else need[by - 1]
        begin = pl.multiple_of(rows * mine, rows) if halved else tokens - count
        behind = by - 1 if halved else 0
        return pltpu.make_async_remote_copy(
            src_ref=even.at[pl.ds(begin + (hops - behind) * tokens, count)],
            dst_ref=even.at[pl.ds(begin + (hops - by) * tokens, count)],
            send_sem=lat_send.at[by - 1],
            recv_sem=lat_recv.at[by - 1],
            device_id=up_by(1 if halved else by),
            device_id_type=MESH,
        )

    def lat_pass(by):
        begin = pl.multiple_of(rows * mine, rows)
        region = even.at[pl.ds(begin + (hops - by) * tokens, rows)]
        return pltpu.make_async_remote_copy(
            src_ref=region,
            dst_ref=even.at[pl.ds(begin + (hops - by) * tokens, rows)],
            send_sem=pass_send.at[by - 1],
            recv_sem=pass_recv.at[by - 1],
            device_id=partner,
            device_id_type=MESH,
        )

    direct = range(1, 2 if halved else hops + 1)
    upper = mine == 1
    sends_on = upper & (place >= 1) & (place + 1 < ctx_count)
    far_comes = place >= 2

    blank = jnp.zeros((tokens, even.shape[1] - width), even.dtype)
    lat_copy.wait()
    even[hops * tokens :] = jnp.concatenate([window[...], blank], axis=1)
    pl.semaphore_wait(barrier, peers)
    for by in direct:

        @pl.when(place + by < ctx_count)
        def _():
            lat_copy_to(by).start()

    mq_copy.start()
    up_copy.start()
    proj_copy.start()

    def state_copy(c):
        part = pl.ds(c * per_pass, per_pass)
        return pltpu.make_async_remote_copy(
            src_ref=state_out.at[part],
            dst_ref=state_in.at[part],
            send_sem=state_send.at[c],
            recv_sem=state_recv.at[c],
            device_id=up_by(1),
            device_id_type=MESH,
        )

    def relay(c, _):
        @pl.when(place > 0)
        def _():
            state_copy(c).wait_recv()

        @pl.when(place == 0)
        def _():
            for n in range(per_pass):
                head = c * per_pass + n
                state_out[head] = offset[head].astype(state_out.dtype)

        @pl.when((place > 0) & (place + 1 < ctx_count))
        def _():
            for n in range(per_pass):
                head = c * per_pass + n
                state_out[head] = (
                    offset[head]
                    + jnp.dot(
                        transition[head], state_in[head], preferred_element_type=jnp.float32
                    )
                ).astype(state_out.dtype)

        @pl.when(place + 1 < ctx_count)
        def _():
            state_copy(c).start()

        return 0

    passes_group = passes // groups

    def relay_slot(time, ready, before):
        due = (time - FIRST_PASS - HOP_LATE * (place - 1)) // PASS_TIME + 1
        due = jnp.where(place == 0, ready, jnp.where(place == ctx_count - 1, 0, due))
        after = jnp.maximum(before, jnp.minimum(due, passes))
        lax.fori_loop(before, after, relay, 0)
        return after

    for by in range(1, hops + 1):

        @pl.when(place < by)
        def _():
            stop = (hops - by + 1) * tokens
            even[stop - need[by - 1] : stop] = jnp.zeros(
                (need[by - 1], even.shape[1]), even.dtype
            )

    lengths_copy.wait()
    strength_copy.wait()
    delta_setup(
        lengths_ref, strength, rel_top, rel_bot, carried, tail, beta, first, per_group
    )
    pos_q = first + iota2((tokens, 1), 0)
    for n in range(2):
        q = slice(n * rows, (n + 1) * rows)
        pos_key = pos_q[n * rows : n * rows + 1] - (key_count - rows) + iota2((1, key_count), 1)
        doc_q, doc_key = jnp.zeros((rows, 1), jnp.int32), jnp.zeros_like(pos_key)
        end = jnp.int32(0)
        for d in range(lengths_ref.shape[1]):
            end = end + lengths_ref[0, d]
            doc_q = doc_q + jnp.where(pos_q[q] >= end, 1, 0)
            doc_key = doc_key + jnp.where(pos_key >= end, 1, 0)
        bias[n] = jnp.where(
            (pos_key <= pos_q[q]) & (pos_key >= 0) & (doc_key == doc_q), 0.0, masked_score
        )

    def pass_latents():
        @pl.when(place >= 1)
        def _():
            lat_copy_to(1).wait_recv()

        @pl.when(sends_on)
        def _():
            lat_copy_to(2).start()

        @pl.when(place >= 1)
        def _():
            lat_pass(1).start()

    def delta_step(g, done):
        for copy in kda_loads(g):
            copy.wait()
        begin = DELTA_AT + DELTA_TIME * g // groups

        def scored(done):
            return relay_slot(begin + DELTA_TIME * 2 // (5 * groups), passes_group * g, done)

        def inverted(done):
            return relay_slot(begin + DELTA_TIME * 3 // (4 * groups), passes_group * g, done)

        def stated(done):
            return relay_slot(begin + DELTA_TIME // groups, passes_group * (g + 1), done)

        done = delta_group(
            g, per_group, kq, kk, kv, kg, beta, rel_top, rel_bot, carried, tail,
            readout, local_part, transition, offset, scored, inverted, stated, done,
        )
        if halved:
            pl.when(g == 0)(pass_latents)

        return done

    done = lax.fori_loop(0, groups, delta_step, jnp.int32(0))

    def shifted(n):
        begin = first_key if n == 0 else 0
        part = slice(n * tokens + begin, (n + 1) * tokens)
        odd[part] = jnp.concatenate([blank[begin:], even[part][:, :width]], axis=1)

    if halved:

        @pl.when(place >= 1)
        def _():
            lat_pass(1).wait_recv()

        @pl.when(upper & far_comes)
        def _():
            lat_copy_to(2).wait_recv()
            lat_pass(2).start()

        @pl.when(upper)
        def _():
            shifted(0)

    else:
        for by in direct:

            @pl.when(place >= by)
            def _():
                lat_copy_to(by).wait_recv()

            shifted(hops - by)

    def last_latents():
        @pl.when(far_comes)
        def _():
            lat_pass(2).wait_recv()

        shifted(0)

    for n in range(1 if halved else hops, hops + 1):
        shifted(n)

    def far_copy(n):
        return pltpu.make_async_remote_copy(
            src_ref=far_send.at[n],
            dst_ref=far_recv.at[n],
            send_sem=far_ssem.at[n],
            recv_sem=far_rsem.at[n],
            device_id=partner,
            device_id_type=MESH,
        )

    far_half = 1 - mine if exchange else 0
    near_half = mine if exchange else 1
    up_copy.wait()
    mq_copy.wait()

    def attention(turn, done):
        half = jnp.where(turn == 0, far_half, near_half)
        if halved:
            pl.when((turn == 1) & (mine == 0))(last_latents)
        time = TURN_AT + turn * (ATTEND_TIME + PROJECT_TIME)

        def attend_turn(step, done):
            attend_step(
                half, step, per_step, mq, even, odd, bias, up, head_out,
                width=width, first_key=first_key, key_count=key_count, score_scale=score_scale,
            )
            return relay_slot(time + ATTEND_TIME * (step + 1) // steps, passes, done)

        done = lax.fori_loop(0, steps, attend_turn, done)

        @pl.when(turn == 0)
        def _():
            proj_copy.wait()

        def project(n, done):
            parts = [
                jnp.dot(
                    head_out[...],
                    proj[:, pl.ds(pl.multiple_of((n * joined + m) * CHUNK, CHUNK), CHUNK)],
                    preferred_element_type=jnp.float32,
                )
                for m in range(joined)
            ]

            @pl.when(turn == 0)
            def _():
                for m in range(joined):
                    far_send[n * joined + m] = parts[m].astype(jnp.bfloat16)
                    if exchange:
                        far_copy(n * joined + m).start()

            @pl.when(turn == 1)
            def _():
                for m in range(joined):
                    near_part[n * joined + m] = parts[m]

            return relay_slot(
                time + ATTEND_TIME + PROJECT_TIME * joined * (n + 1) // pieces, passes, done
            )

        return lax.fori_loop(0, pieces // joined, project, done)

    done = lax.fori_loop(0, 2, attention, done)

    def read_heads(c, _):
        @pl.when(c >= done)
        def _():
            relay(c, 0)

        for n in range(per_pass):
            head = c * per_pass + n
            at = pl.ds(pl.multiple_of(head * state_dim, state_dim), state_dim)

            @pl.when(place > 0)
            def _():
                kda_stage[0, :, at] = (
                    local_part[:, at]
                    + jnp.dot(readout[:, at], state_in[head], preferred_element_type=jnp.float32)
                ).astype(kda_stage.dtype)

            @pl.when(place == 0)
            def _():
                kda_stage[0, :, at] = local_part[:, at].astype(kda_stage.dtype)

        return 0

    lax.fori_loop(0, passes, read_heads, 0)

    def mix(n, _):
        at = pl.ds(pl.multiple_of(n * CHUNK, CHUNK), CHUNK)
        if exchange:
            far_copy(n).wait_recv()
            mixed_stage[0, :, at] = (near_part[n] + far_recv[n].astype(jnp.float32)).astype(
                jnp.bfloat16
            )
        else:
            mixed_stage[0, :rows, at] = far_send[n]
            mixed_stage[0, rows:, at] = near_part[n].astype(jnp.bfloat16)
        return 0

    lax.fori_loop(0, pieces, mix, 0)

    for by in direct:

        @pl.when(place + by < ctx_count)
        def _():
            lat_copy_to(by).wait_send()

    if halved:

        @pl.when(place >= 1)
        def _():
            lat_pass(1).wait_send()

        @pl.when(sends_on)
        def _():
            lat_copy_to(2).wait_send()

        @pl.when(upper & far_comes)
        def _():
            lat_pass(2).wait_send()

    @pl.when(place + 1 < ctx_count)
    def _():
        for c in range(passes):
            state_copy(c).wait_send()

    if exchange:
        for n in range(pieces):
            far_copy(n).wait_send()


def write_out(kda_ref, mixed_ref, kda_hbm, mixed_hbm, sem):
    copies = [
        pltpu.make_async_copy(kda_ref, kda_hbm, sem.at[0]),
        pltpu.make_async_copy(mixed_ref, mixed_hbm, sem.at[1]),
    ]
    for copy in copies:
        copy.start()
    for copy in copies:
        copy.wait()


def local(
    kda_query, kda_key, kda_value, log_decay, write_strength, mla_query, latents, value_up,
    out_proj, doc_lengths,
):
    tokens = kda_query.shape[1]
    heads = write_strength.shape[1]
    lanes = kda_query.shape[2]
    state_dim = lanes // heads
    ctx_count = lax.axis_size("ctx")
    head_count = lax.axis_size("head")
    exchange = head_count == 2
    longest = 3 * tokens * ctx_count // 8
    hops = min(ctx_count - 1, -(-(longest - 1) // tokens))
    width = latents.shape[2]
    spare = -width % 128
    model = out_proj.shape[1]
    rows = tokens // 2
    back = -(-(longest - 1) // rows) * rows
    first_key = hops * tokens - back
    need = [min(tokens, back - (by - 1) * tokens) for by in range(1, hops + 1)]
    per_group = math.gcd(heads, 8)
    per_step = math.gcd(heads, 8)
    per_pass = 2
    top = 2 * (tokens // 3)
    wide = 2 * top
    groups, steps, passes, pieces = (
        heads // per_group, heads // per_step, heads // per_pass, model // CHUNK,
    )
    window_rows = (hops + 1) * tokens
    bf16, f32 = jnp.bfloat16, jnp.float32
    vmem = pltpu.VMEM
    dma = pltpu.SemaphoreType.DMA
    scratch = [
        pltpu.SMEM(doc_lengths.shape, jnp.int32),
        vmem((tokens, lanes), bf16),
        vmem((tokens, lanes), bf16),
        vmem((tokens, lanes), bf16),
        vmem((tokens, lanes), bf16),
        vmem((heads, tokens), f32),
        vmem((tokens, heads * width), bf16),
        vmem((tokens, width), bf16),
        vmem((window_rows, width + spare), bf16),
        vmem((window_rows, width + spare), bf16),
        vmem(value_up.shape, bf16),
        vmem(out_proj.shape, bf16),
        vmem((top, top), jnp.int32),
        vmem((tokens - top, wide), jnp.int32),
        vmem((tokens, state_dim), f32),
        vmem((tokens, state_dim), f32),
        vmem((groups, tokens, 128), f32),
        vmem((tokens, lanes), bf16),
        vmem((tokens, lanes), f32),
        vmem((heads, state_dim, state_dim), bf16),
        vmem((heads, state_dim, state_dim), f32),
        vmem((heads, state_dim, state_dim), bf16),
        vmem((heads, state_dim, state_dim), bf16),
        vmem((2, rows, back + rows), f32),
        vmem((rows, heads * value_up.shape[2]), bf16),
        vmem((pieces, rows, CHUNK), bf16),
        vmem((pieces, rows, CHUNK), bf16),
        vmem((pieces, rows, CHUNK), f32),
        dma((groups, 4)),
        dma((6,)),
        dma((hops,)),
        dma((hops,)),
        dma((hops,)),
        dma((hops,)),
        dma((passes,)),
        dma((passes,)),
        dma((pieces,)),
        dma((pieces,)),
    ]
    anywhere = pl.BlockSpec(memory_space=pl.ANY)
    kda_out, mixed = pl.pallas_call(
        functools.partial(
            layers, hops=hops, need=need, width=width, per_group=per_group, per_step=per_step,
            per_pass=per_pass, first_key=first_key, key_count=back + rows,
            score_scale=1.0 / math.sqrt(NOPE + ROPE), exchange=exchange,
        ),
        in_specs=[anywhere] * 10,
        out_specs=[pl.BlockSpec(memory_space=pltpu.VMEM)] * 2,
        out_shape=[
            pltpu.VMEM((1, tokens, lanes), bf16),
            pltpu.VMEM((1, rows if exchange else tokens, model), bf16),
        ],
        scratch_shapes=scratch,
        compiler_params=pltpu.CompilerParams(
            vmem_limit_bytes=58 << 20, collective_id=0, has_side_effects=True
        ),
        cost_estimate=pl.CostEstimate(
            flops=10_000_000_000, bytes_accessed=20_000_000, transcendentals=0
        ),
    )(
        in_place(doc_lengths), in_place(kda_query), in_place(kda_key), in_place(kda_value),
        in_place(log_decay), in_place(write_strength), in_place(mla_query), in_place(latents),
        in_place(value_up), in_place(out_proj),
    )
    if not exchange:
        mixed = lax.psum_scatter(mixed, "head", scatter_dimension=1, tiled=True)
        return kda_out, mixed
    return pl.pallas_call(
        write_out,
        in_specs=[pl.BlockSpec(memory_space=pltpu.VMEM)] * 2,
        out_specs=[anywhere] * 2,
        out_shape=[pltpu.HBM(kda_out.shape, bf16), pltpu.HBM(mixed.shape, bf16)],
        scratch_shapes=[dma((2,))],
        compiler_params=pltpu.CompilerParams(vmem_limit_bytes=4 << 20),
    )(
        pltpu.with_memory_space_constraint(kda_out, pltpu.VMEM),
        pltpu.with_memory_space_constraint(mixed, pltpu.VMEM),
    )


def solution(mesh):
    placed = (
        P(("group", "req"), "ctx", "head"),
        P(("group", "req"), "ctx", "head"),
        P(("group", "req"), "ctx", "head"),
        P(("group", "req"), "ctx", "head"),
        P(("group", "req"), "head", "ctx"),
        P(("group", "req"), "ctx", "head"),
        P(("group", "req"), "ctx", None),
        P("head", None, None),
        P("head", None),
        P(("group", "req"), None),
    )
    return jax.shard_map(
        local,
        mesh=mesh,
        in_specs=placed,
        out_specs=(P(("group", "req"), "ctx", "head"), P(("group", "req"), ("ctx", "head"), None)),
        check_vma=False,
    )
```

```python
import functools
import math

import jax
import jax.numpy as jnp
from jax import lax
from jax.experimental import pallas as pl
from jax.experimental.pallas import tpu as pltpu
from jax.sharding import PartitionSpec as P

ROPE = 64
NOPE = 128
MESH = pl.DeviceIdType.MESH
CHUNK = 256

DELTA_AT = 26
DELTA_TIME = 78
TURN_AT = 107
ATTEND_TIME = 35
PROJECT_TIME = 28
FIRST_PASS = 87
HOP_LATE = 39
PASS_TIME = 14

masked_score = -1e30
ROWS = (((1,), (0,)), ((), ()))
TRANS = (((1,), (1,)), ((), ()))
OVER = (((0,), (0,)), ((), ()))


def in_place(value):
    return pltpu.with_memory_space_constraint(value, pltpu.HBM)


def dot_once(left, right, dims):
    return lax.dot_general(
        left.astype(jnp.bfloat16),
        right.astype(jnp.bfloat16),
        dims,
        preferred_element_type=jnp.float32,
    )


def iota2(shape, axis):
    return lax.broadcasted_iota(jnp.int32, shape, axis)


def delta_setup(lengths_ref, strength_ref, rel_top, rel_bot, carried_ref, tail_ref, beta_ref, first, per_group):
    tokens, state_dim = carried_ref.shape
    top = rel_top.shape[0]
    wide = rel_bot.shape[1]
    bot = tokens - top
    pos_col = first + iota2((tokens, 1), 0)
    pos_row = first + iota2((1, wide), 1)
    doc_col, doc_row = jnp.zeros_like(pos_col), jnp.zeros_like(pos_row)
    prev_doc, last_doc, end = jnp.int32(0), jnp.int32(0), jnp.int32(0)
    for d in range(lengths_ref.shape[1]):
        end = end + lengths_ref[0, d]
        doc_col = doc_col + jnp.where(pos_col >= end, 1, 0)
        doc_row = doc_row + jnp.where(pos_row >= end, 1, 0)
        prev_doc = prev_doc + jnp.where(first - 1 >= end, 1, 0)
        last_doc = last_doc + jnp.where(first + tokens - 1 >= end, 1, 0)
    rel_top[...] = jnp.where(
        doc_col[:top] == doc_row[:, :top], iota2((top, top), 0) - iota2((top, top), 1), -1
    )
    rel_bot[...] = jnp.where(
        (doc_col[top:] == doc_row) & (iota2((bot, wide), 1) < tokens),
        iota2((bot, wide), 0) + top - iota2((bot, wide), 1),
        -1,
    )
    ones = jnp.ones((1, state_dim), jnp.float32)
    carried_ref[...] = jnp.where(doc_col == prev_doc, 1.0, 0.0) * ones
    tail_ref[...] = jnp.where(doc_col == last_doc, 1.0, 0.0) * ones
    heads = strength_ref.shape[0]
    padded = jnp.concatenate(
        [strength_ref[...], jnp.zeros((heads, wide - tokens), jnp.float32)], axis=1
    )
    padded = jnp.concatenate([padded, jnp.zeros((128 - heads, wide), jnp.float32)], axis=0)
    turned = jnp.transpose(padded)[:tokens]
    for g in range(heads // per_group):
        beta_ref[g] = turned if g == 0 else pltpu.roll(turned, 128 - g * per_group, 1)


def packed_inverse(pack):
    lane = iota2((1, 128), 1)
    piece = pack[0:16]
    for b in range(1, 4):
        piece = jnp.where((lane % 64) // 16 == b, pack[16 * b : 16 * b + 16], piece)
    row16, col16 = iota2((16, 128), 0), iota2((16, 128), 1) % 16
    inv = jnp.where((row16 // 2 == col16 // 2) & (row16 > col16), -piece, 0.0)
    yield
    for width, size in ((2, 16), (4, 16), (8, 16), (16, 32), (32, 64)):
        if size == 32:
            piece = jnp.where((lane % 64) // 32 == 0, pack[0:32], pack[32:64])
        elif size == 64:
            piece = pack
        if width == size // 2 and size > 16:
            inv = jnp.concatenate(
                [
                    jnp.where(lane % size < width, inv, 0.0),
                    jnp.where(lane % size >= width, inv, 0.0),
                ],
                axis=0,
            )
        row, col = iota2((size, 128), 0), iota2((size, 128), 1) % size
        corner = (row // (2 * width) == col // (2 * width)) & (row // width > col // width)
        part = jnp.where(corner, piece, 0.0)
        left = part + dot_once(inv, spread(part, size), ROWS)
        yield
        inv = inv - (left + dot_once(left, spread(inv, size), ROWS))
        yield
    yield inv


def spread(cells, size):
    copies = 128 // size
    own = iota2((128, 128), 0) // size == iota2((128, 128), 1) // size
    return jnp.where(own, jnp.concatenate([cells] * copies, axis=0), 0.0).astype(jnp.bfloat16)


def together(makers):
    done = []
    while True:
        step = [next(m) for m in makers]
        if step[0] is not None:
            return step


def delta_group(
    g, per_group, query_ref, key_ref, value_ref, decay_ref, beta_ref, rel_top, rel_bot,
    carried_ref, tail_ref, readout_ref, local_ref, transition_ref, offset_ref,
    inverted, stated, done,
):
    tokens, state_dim = carried_ref.shape
    top = rel_top.shape[0]
    half = top // 2
    heads = range(per_group)
    inclusive = jnp.where(
        iota2((tokens, tokens), 0) >= iota2((tokens, tokens), 1), 1.0, 0.0
    ).astype(jnp.bfloat16)
    lane = iota2((1, 128), 1)
    at = [
        pl.ds(pl.multiple_of((g * per_group + h) * state_dim, state_dim), state_dim) for h in heads
    ]
    summed = []
    for h in range(0, per_group, 2):
        both = pl.ds(
            pl.multiple_of((g * per_group + h) * state_dim, 2 * state_dim), 2 * state_dim
        )
        pair = jnp.dot(inclusive, decay_ref[:, both], preferred_element_type=jnp.float32)
        summed += [pair[:, :state_dim], pair[:, state_dim:]]
    lower_top, lower_bot, attend_top, attend_bot = [], [], [], []
    right_keys, read_query, key_decay, kept, rights = [], [], [], [], []
    for h in heads:
        s = summed[h]
        query = query_ref[:, at[h]].astype(jnp.float32)
        key = key_ref[:, at[h]].astype(jnp.float32)
        beta = beta_ref[g, :, h : h + 1]
        query = query * lax.rsqrt(jnp.sum(query * query, axis=1, keepdims=True) + 1e-06)
        key = key * lax.rsqrt(jnp.sum(key * key, axis=1, keepdims=True) + 1e-06)
        written = key * beta
        mid, start, last = s[half - 1 : half], s[top - 1 : top], s[tokens - 1 : tokens]
        fall_top, fall_bot = jnp.exp(s[:top] - mid), jnp.exp(s[top:] - start)
        lift_top, lift_bot = jnp.exp(mid - s[:top]), jnp.exp(start - s[top:])
        to_mid, to_start, mid_start = jnp.exp(mid), jnp.exp(start), jnp.exp(start - mid)
        key_top, key_bot = written[:top] * fall_top, written[top:] * fall_bot
        query_top, query_bot = query[:top] * fall_top, query[top:] * fall_bot
        raised_top = key[:top] * lift_top
        raised_all = jnp.concatenate([raised_top * mid_start, key[top:] * lift_bot], axis=0)
        both_top = dot_once(
            jnp.concatenate([key_top, query_top], axis=0), raised_top, TRANS
        )
        both_bot = dot_once(
            jnp.concatenate([key_bot, query_bot], axis=0),
            jnp.concatenate([raised_all, jnp.zeros((half, state_dim), jnp.float32)], axis=0),
            TRANS,
        )
        lower_top.append(jnp.where(rel_top[...] > 0, both_top[:top], 0.0))
        attend_top.append(jnp.where(rel_top[...] >= 0, both_top[top:], 0.0).astype(jnp.bfloat16))
        lower_bot.append(jnp.where(rel_bot[...] > 0, both_bot[:half], 0.0))
        attend_bot.append(
            jnp.where(rel_bot[...] >= 0, both_bot[half:], 0.0).astype(jnp.bfloat16)
        )
        carried = carried_ref[...]
        grown = jnp.concatenate([key_top * to_mid, key_bot * to_start], axis=0) * carried
        read_query.append(
            jnp.concatenate([query_top * to_mid, query_bot * to_start], axis=0) * carried
        )
        key_decay.append((raised_all * jnp.exp(last - start) * tail_ref[...]).astype(jnp.bfloat16))
        kept.append(jnp.exp(last) * carried[tokens - 1 : tokens])
        rights.append(
            jnp.concatenate([grown, value_ref[:, at[h]].astype(jnp.float32) * beta], axis=1)
        )
    makers = [
        packed_inverse(jnp.where(lane < half, lower_top[h][:half], lower_top[h][half:]))
        for h in heads
    ]
    makers += [
        packed_inverse(
            jnp.where(
                lane < half,
                lower_bot[h][:, top:],
                pltpu.roll(lower_bot[h + 1][:, top:], half, 1),
            )
        )
        for h in range(0, per_group, 2)
    ]
    inverses = together(makers)
    done = inverted(done)
    firsts, seconds, tops, wholes = [], [], [], []
    for h in heads:
        right = rights[h]
        inv = jnp.where(lane < half, inverses[h], 0.0)
        firsts.append(right[:half] + dot_once(inv, right[:top], ROWS))
    for h in heads:
        across = jnp.where(lane < half, lower_top[h][half:], 0.0)
        seconds.append(
            rights[h][half:top]
            - dot_once(across, jnp.concatenate([firsts[h]] * 2, axis=0), ROWS)
        )
    for h in heads:
        inv = jnp.where(lane >= half, inverses[h], 0.0)
        tops.append(
            jnp.concatenate(
                [
                    firsts[h],
                    seconds[h] + dot_once(inv, jnp.concatenate([seconds[h]] * 2, axis=0), ROWS),
                ],
                axis=0,
            ).astype(jnp.bfloat16)
        )
    thirds = [
        rights[h][top:] - dot_once(lower_bot[h][:, :top], tops[h], ROWS) for h in heads
    ]
    for h in heads:
        inv = inverses[per_group + h // 2]
        inv = jnp.where(lane < half, inv, 0.0) if h % 2 == 0 else jnp.where(lane >= half, inv, 0.0)
        third = thirds[h] + dot_once(inv, jnp.concatenate([thirds[h]] * 2, axis=0), ROWS)
        wholes.append(jnp.concatenate([tops[h], third.astype(jnp.bfloat16)], axis=0))
    eye = iota2((state_dim, state_dim), 0) == iota2((state_dim, state_dim), 1)
    for h in heads:
        moved = dot_once(key_decay[h], wholes[h], OVER)
        head = g * per_group + h
        transition_ref[head] = (
            jnp.where(eye, kept[h], 0.0) - moved[:, :state_dim]
        ).astype(transition_ref.dtype)
        offset_ref[head] = moved[:, state_dim:]
    done = stated(done)
    for h in heads:
        read = dot_once(attend_top[h], tops[h], ROWS)
        readout_ref[:top, at[h]] = (read_query[h][:top] - read[:, :state_dim]).astype(
            readout_ref.dtype
        )
        local_ref[:top, at[h]] = read[:, state_dim:]
        read = dot_once(attend_bot[h][:, :tokens], wholes[h], ROWS)
        readout_ref[top:, at[h]] = (read_query[h][top:] - read[:, :state_dim]).astype(
            readout_ref.dtype
        )
        local_ref[top:, at[h]] = read[:, state_dim:]
    return done


def attend_step(
    half, step, group, query_ref, even_ref, odd_ref, bias_ref, up_ref, out_ref,
    *, width, first_key, key_count, score_scale,
):
    rows = out_ref.shape[0]
    wide = even_ref.shape[1]
    lat_dim, vhead = up_ref.shape[1:]
    pairs = group // 2
    keys = pl.ds(pl.multiple_of(half * rows + first_key, math.gcd(rows, first_key)), key_count)
    own = pl.ds(pl.multiple_of(half * rows, rows), rows)
    bias = bias_ref[half]
    contexts = []
    for key_ref, skip in ((even_ref, 0), (odd_ref, 2 * width - wide)):
        stacked = []
        for p in range(pairs):
            begin = (step * group + 2 * p) * width + skip
            stacked.append(query_ref[own, pl.ds(pl.multiple_of(begin, 128), wide)])
        query = jnp.concatenate(stacked, axis=0) if pairs > 1 else stacked[0]
        scores = lax.dot_general(
            query, key_ref[keys, :], TRANS, preferred_element_type=jnp.float32
        )
        scores = scores.reshape(pairs, rows, key_count) * score_scale + bias[None]
        exponent = jnp.exp(scores - jnp.max(scores, axis=2, keepdims=True))
        exponent = exponent.reshape(pairs * rows, key_count)
        row_total = jnp.sum(exponent, axis=1, keepdims=True)
        weighted = jnp.dot(
            exponent.astype(jnp.bfloat16),
            even_ref[keys, :lat_dim],
            preferred_element_type=jnp.float32,
        )
        contexts.append((weighted / row_total).astype(jnp.bfloat16))
    for p in range(pairs):
        for parity in range(2):
            head = step * group + 2 * p + parity
            out_ref[:, pl.ds(pl.multiple_of(head * vhead, vhead), vhead)] = jnp.dot(
                contexts[parity][p * rows : (p + 1) * rows],
                up_ref[head],
                preferred_element_type=jnp.float32,
            ).astype(jnp.bfloat16)


def layers(
    lengths_hbm, kq_hbm, kk_hbm, kv_hbm, kg_hbm, strength_hbm, mq_hbm, lat_hbm, up_hbm, proj_hbm,
    kda_stage, mixed_stage,
    lengths_ref, kq, kk, kv, kg, strength, mq, window, even, odd, up, proj,
    rel_top, rel_bot, carried, tail, beta, readout, local_part, transition, offset,
    state_out, state_in, bias, head_out, far_send, far_recv, near_part,
    kda_sem, load_sem, lat_send, lat_recv, pass_send, pass_recv,
    state_send, state_recv, far_ssem, far_rsem,
    *, hops, need, width, per_group, per_step, per_pass, first_key, key_count, score_scale, exchange,
):
    tokens, lanes = kq.shape
    heads = strength.shape[0]
    state_dim = lanes // heads
    groups = heads // per_group
    steps = heads // per_step
    passes = heads // per_pass
    rows = tokens // 2
    ctx_count = lax.axis_size("ctx")
    place = lax.axis_index("ctx")
    mine = lax.axis_index("head")
    model = proj.shape[1]
    pieces = model // CHUNK
    joined = math.gcd(pieces, 3)
    first = place * tokens

    def up_by(by):
        return {"ctx": place + by}

    partner = {"head": 1 - mine}

    def load(source, target, sem):
        return pltpu.make_async_copy(source, target, sem)

    def kda_loads(g):
        part = pl.ds(pl.multiple_of(g * per_group * state_dim, state_dim), per_group * state_dim)
        return [
            load(source.at[0, :, part], target.at[:, part], kda_sem.at[g, n])
            for n, (source, target) in enumerate(
                ((kg_hbm, kg), (kq_hbm, kq), (kk_hbm, kk), (kv_hbm, kv))
            )
        ]

    strength_copy = load(strength_hbm.at[0], strength, load_sem.at[0])
    lat_copy = load(lat_hbm.at[0], window, load_sem.at[1])
    mq_copy = load(mq_hbm.at[0], mq, load_sem.at[2])
    up_copy = load(up_hbm, up, load_sem.at[3])
    proj_copy = load(proj_hbm, proj, load_sem.at[4])
    lengths_copy = load(lengths_hbm, lengths_ref, load_sem.at[5])

    barrier = pltpu.get_barrier_semaphore()
    halved = exchange and hops == 2 and need == [tokens, rows]
    peers = jnp.int32(0)
    for by in range(1, 2 if halved else hops + 1):
        for sign in (1, -1):
            there = place + sign * by
            known = (there >= 0) & (there < ctx_count)
            peers = peers + jnp.where(known, 1, 0)

            @pl.when(known)
            def _():
                pl.semaphore_signal(
                    barrier, inc=1, device_id={"ctx": there}, device_id_type=MESH
                )

    if exchange:
        pl.semaphore_signal(barrier, inc=1, device_id=partner, device_id_type=MESH)
        peers = peers + 1

    lat_copy.start()
    lengths_copy.start()
    strength_copy.start()
    for g in range(groups):
        for copy in kda_loads(g):
            copy.start()


    def lat_copy_to(by):
        count = rows if halved else need[by - 1]
        begin = pl.multiple_of(rows * mine, rows) if halved else tokens - count
        behind = by - 1 if halved else 0
        return pltpu.make_async_remote_copy(
            src_ref=even.at[pl.ds(begin + (hops - behind) * tokens, count)],
            dst_ref=even.at[pl.ds(begin + (hops - by) * tokens, count)],
            send_sem=lat_send.at[by - 1],
            recv_sem=lat_recv.at[by - 1],
            device_id=up_by(1 if halved else by),
            device_id_type=MESH,
        )

    def lat_pass(by):
        begin = pl.multiple_of(rows * mine, rows)
        region = even.at[pl.ds(begin + (hops - by) * tokens, rows)]
        return pltpu.make_async_remote_copy(
            src_ref=region,
            dst_ref=even.at[pl.ds(begin + (hops - by) * tokens, rows)],
            send_sem=pass_send.at[by - 1],
            recv_sem=pass_recv.at[by - 1],
            device_id=partner,
            device_id_type=MESH,
        )

    direct = range(1, 2 if halved else hops + 1)
    upper = mine == 1
    sends_on = upper & (place >= 1) & (place + 1 < ctx_count)
    far_comes = place >= 2

    blank = jnp.zeros((tokens, even.shape[1] - width), even.dtype)
    lat_copy.wait()
    even[hops * tokens :] = jnp.concatenate([window[...], blank], axis=1)
    pl.semaphore_wait(barrier, peers)
    for by in direct:

        @pl.when(place + by < ctx_count)
        def _():
            lat_copy_to(by).start()

    mq_copy.start()
    up_copy.start()
    proj_copy.start()

    def state_copy(c):
        part = pl.ds(c * per_pass, per_pass)
        return pltpu.make_async_remote_copy(
            src_ref=state_out.at[part],
            dst_ref=state_in.at[part],
            send_sem=state_send.at[c],
            recv_sem=state_recv.at[c],
            device_id=up_by(1),
            device_id_type=MESH,
        )

    def relay(c, _):
        @pl.when(place > 0)
        def _():
            state_copy(c).wait_recv()

        @pl.when(place == 0)
        def _():
            for n in range(per_pass):
                head = c * per_pass + n
                state_out[head] = offset[head].astype(state_out.dtype)

        @pl.when((place > 0) & (place + 1 < ctx_count))
        def _():
            for n in range(per_pass):
                head = c * per_pass + n
                state_out[head] = (
                    offset[head]
                    + jnp.dot(
                        transition[head], state_in[head], preferred_element_type=jnp.float32
                    )
                ).astype(state_out.dtype)

        @pl.when(place + 1 < ctx_count)
        def _():
            state_copy(c).start()

        return 0

    passes_group = passes // groups

    def relay_slot(time, ready, before):
        due = (time - FIRST_PASS - HOP_LATE * (place - 1)) // PASS_TIME + 1
        due = jnp.where(place == 0, ready, jnp.where(place == ctx_count - 1, 0, due))
        after = jnp.maximum(before, jnp.minimum(due, passes))
        lax.fori_loop(before, after, relay, 0)
        return after

    for by in range(1, hops + 1):

        @pl.when(place < by)
        def _():
            stop = (hops - by + 1) * tokens
            even[stop - need[by - 1] : stop] = jnp.zeros(
                (need[by - 1], even.shape[1]), even.dtype
            )

    lengths_copy.wait()
    strength_copy.wait()
    delta_setup(
        lengths_ref, strength, rel_top, rel_bot, carried, tail, beta, first, per_group
    )
    pos_q = first + iota2((tokens, 1), 0)
    for n in range(2):
        q = slice(n * rows, (n + 1) * rows)
        pos_key = pos_q[n * rows : n * rows + 1] - (key_count - rows) + iota2((1, key_count), 1)
        doc_q, doc_key = jnp.zeros((rows, 1), jnp.int32), jnp.zeros_like(pos_key)
        end = jnp.int32(0)
        for d in range(lengths_ref.shape[1]):
            end = end + lengths_ref[0, d]
            doc_q = doc_q + jnp.where(pos_q[q] >= end, 1, 0)
            doc_key = doc_key + jnp.where(pos_key >= end, 1, 0)
        bias[n] = jnp.where(
            (pos_key <= pos_q[q]) & (pos_key >= 0) & (doc_key == doc_q), 0.0, masked_score
        )

    def pass_latents():
        @pl.when(place >= 1)
        def _():
            lat_copy_to(1).wait_recv()

        @pl.when(sends_on)
        def _():
            lat_copy_to(2).start()

        @pl.when(place >= 1)
        def _():
            lat_pass(1).start()

    def delta_step(g, done):
        for copy in kda_loads(g):
            copy.wait()
        begin = DELTA_AT + DELTA_TIME * g // groups

        def inverted(done):
            return relay_slot(begin + DELTA_TIME * 3 // (4 * groups), passes_group * g, done)

        def stated(done):
            return relay_slot(begin + DELTA_TIME // groups, passes_group * (g + 1), done)

        done = delta_group(
            g, per_group, kq, kk, kv, kg, beta, rel_top, rel_bot, carried, tail,
            readout, local_part, transition, offset, inverted, stated, done,
        )
        if halved:
            pl.when(g == 0)(pass_latents)

        return done

    done = lax.fori_loop(0, groups, delta_step, jnp.int32(0))

    def shifted(n):
        begin = first_key if n == 0 else 0
        part = slice(n * tokens + begin, (n + 1) * tokens)
        odd[part] = jnp.concatenate([blank[begin:], even[part][:, :width]], axis=1)

    if halved:

        @pl.when(place >= 1)
        def _():
            lat_pass(1).wait_recv()

        @pl.when(upper & far_comes)
        def _():
            lat_copy_to(2).wait_recv()
            lat_pass(2).start()

        @pl.when(upper)
        def _():
            shifted(0)

    else:
        for by in direct:

            @pl.when(place >= by)
            def _():
                lat_copy_to(by).wait_recv()

            shifted(hops - by)

    def last_latents():
        @pl.when(far_comes)
        def _():
            lat_pass(2).wait_recv()

        shifted(0)

    for n in range(1 if halved else hops, hops + 1):
        shifted(n)

    def far_copy(n):
        return pltpu.make_async_remote_copy(
            src_ref=far_send.at[n],
            dst_ref=far_recv.at[n],
            send_sem=far_ssem.at[n],
            recv_sem=far_rsem.at[n],
            device_id=partner,
            device_id_type=MESH,
        )

    far_half = 1 - mine if exchange else 0
    near_half = mine if exchange else 1
    up_copy.wait()
    mq_copy.wait()

    def attention(turn, done):
        half = jnp.where(turn == 0, far_half, near_half)
        if halved:
            pl.when((turn == 1) & (mine == 0))(last_latents)
        time = TURN_AT + turn * (ATTEND_TIME + PROJECT_TIME)

        def attend_turn(step, done):
            attend_step(
                half, step, per_step, mq, even, odd, bias, up, head_out,
                width=width, first_key=first_key, key_count=key_count, score_scale=score_scale,
            )
            return relay_slot(time + ATTEND_TIME * (step + 1) // steps, passes, done)

        done = lax.fori_loop(0, steps, attend_turn, done)

        @pl.when(turn == 0)
        def _():
            proj_copy.wait()

        def project(n, done):
            parts = [
                jnp.dot(
                    head_out[...],
                    proj[:, pl.ds(pl.multiple_of((n * joined + m) * CHUNK, CHUNK), CHUNK)],
                    preferred_element_type=jnp.float32,
                )
                for m in range(joined)
            ]

            @pl.when(turn == 0)
            def _():
                for m in range(joined):
                    far_send[n * joined + m] = parts[m].astype(jnp.bfloat16)
                    if exchange:
                        far_copy(n * joined + m).start()

            @pl.when(turn == 1)
            def _():
                for m in range(joined):
                    near_part[n * joined + m] = parts[m]

            return relay_slot(
                time + ATTEND_TIME + PROJECT_TIME * joined * (n + 1) // pieces, passes, done
            )

        return lax.fori_loop(0, pieces // joined, project, done)

    done = lax.fori_loop(0, 2, attention, done)

    def read_heads(c, _):
        @pl.when(c >= done)
        def _():
            relay(c, 0)

        for n in range(per_pass):
            head = c * per_pass + n
            at = pl.ds(pl.multiple_of(head * state_dim, state_dim), state_dim)

            @pl.when(place > 0)
            def _():
                kda_stage[0, :, at] = (
                    local_part[:, at]
                    + jnp.dot(readout[:, at], state_in[head], preferred_element_type=jnp.float32)
                ).astype(kda_stage.dtype)

            @pl.when(place == 0)
            def _():
                kda_stage[0, :, at] = local_part[:, at].astype(kda_stage.dtype)

        return 0

    lax.fori_loop(0, passes, read_heads, 0)

    def mix(n, _):
        at = pl.ds(pl.multiple_of(n * CHUNK, CHUNK), CHUNK)
        if exchange:
            far_copy(n).wait_recv()
            mixed_stage[0, :, at] = (near_part[n] + far_recv[n].astype(jnp.float32)).astype(
                jnp.bfloat16
            )
        else:
            mixed_stage[0, :rows, at] = far_send[n]
            mixed_stage[0, rows:, at] = near_part[n].astype(jnp.bfloat16)
        return 0

    lax.fori_loop(0, pieces, mix, 0)

    for by in direct:

        @pl.when(place + by < ctx_count)
        def _():
            lat_copy_to(by).wait_send()

    if halved:

        @pl.when(place >= 1)
        def _():
            lat_pass(1).wait_send()

        @pl.when(sends_on)
        def _():
            lat_copy_to(2).wait_send()

        @pl.when(upper & far_comes)
        def _():
            lat_pass(2).wait_send()

    @pl.when(place + 1 < ctx_count)
    def _():
        for c in range(passes):
            state_copy(c).wait_send()

    if exchange:
        for n in range(pieces):
            far_copy(n).wait_send()


def write_out(kda_ref, mixed_ref, kda_hbm, mixed_hbm, sem):
    copies = [
        pltpu.make_async_copy(kda_ref, kda_hbm, sem.at[0]),
        pltpu.make_async_copy(mixed_ref, mixed_hbm, sem.at[1]),
    ]
    for copy in copies:
        copy.start()
    for copy in copies:
        copy.wait()


def local(
    kda_query, kda_key, kda_value, log_decay, write_strength, mla_query, latents, value_up,
    out_proj, doc_lengths,
):
    tokens = kda_query.shape[1]
    heads = write_strength.shape[1]
    lanes = kda_query.shape[2]
    state_dim = lanes // heads
    ctx_count = lax.axis_size("ctx")
    head_count = lax.axis_size("head")
    exchange = head_count == 2
    longest = 3 * tokens * ctx_count // 8
    hops = min(ctx_count - 1, -(-(longest - 1) // tokens))
    width = latents.shape[2]
    spare = -width % 128
    model = out_proj.shape[1]
    rows = tokens // 2
    back = -(-(longest - 1) // rows) * rows
    first_key = hops * tokens - back
    need = [min(tokens, back - (by - 1) * tokens) for by in range(1, hops + 1)]
    per_group = math.gcd(heads, 8)
    per_step = math.gcd(heads, 8)
    per_pass = 2
    top = 2 * (tokens // 3)
    wide = 2 * top
    groups, steps, passes, pieces = (
        heads // per_group, heads // per_step, heads // per_pass, model // CHUNK,
    )
    window_rows = (hops + 1) * tokens
    bf16, f32 = jnp.bfloat16, jnp.float32
    vmem = pltpu.VMEM
    dma = pltpu.SemaphoreType.DMA
    scratch = [
        pltpu.SMEM(doc_lengths.shape, jnp.int32),
        vmem((tokens, lanes), bf16),
        vmem((tokens, lanes), bf16),
        vmem((tokens, lanes), bf16),
        vmem((tokens, lanes), bf16),
        vmem((heads, tokens), f32),
        vmem((tokens, heads * width), bf16),
        vmem((tokens, width), bf16),
        vmem((window_rows, width + spare), bf16),
        vmem((window_rows, width + spare), bf16),
        vmem(value_up.shape, bf16),
        vmem(out_proj.shape, bf16),
        vmem((top, top), jnp.int32),
        vmem((tokens - top, wide), jnp.int32),
        vmem((tokens, state_dim), f32),
        vmem((tokens, state_dim), f32),
        vmem((groups, tokens, 128), f32),
        vmem((tokens, lanes), bf16),
        vmem((tokens, lanes), f32),
        vmem((heads, state_dim, state_dim), bf16),
        vmem((heads, state_dim, state_dim), f32),
        vmem((heads, state_dim, state_dim), bf16),
        vmem((heads, state_dim, state_dim), bf16),
        vmem((2, rows, back + rows), f32),
        vmem((rows, heads * value_up.shape[2]), bf16),
        vmem((pieces, rows, CHUNK), bf16),
        vmem((pieces, rows, CHUNK), bf16),
        vmem((pieces, rows, CHUNK), f32),
        dma((groups, 4)),
        dma((6,)),
        dma((hops,)),
        dma((hops,)),
        dma((hops,)),
        dma((hops,)),
        dma((passes,)),
        dma((passes,)),
        dma((pieces,)),
        dma((pieces,)),
    ]
    anywhere = pl.BlockSpec(memory_space=pl.ANY)
    kda_out, mixed = pl.pallas_call(
        functools.partial(
            layers, hops=hops, need=need, width=width, per_group=per_group, per_step=per_step,
            per_pass=per_pass, first_key=first_key, key_count=back + rows,
            score_scale=1.0 / math.sqrt(NOPE + ROPE), exchange=exchange,
        ),
        in_specs=[anywhere] * 10,
        out_specs=[pl.BlockSpec(memory_space=pltpu.VMEM)] * 2,
        out_shape=[
            pltpu.VMEM((1, tokens, lanes), bf16),
            pltpu.VMEM((1, rows if exchange else tokens, model), bf16),
        ],
        scratch_shapes=scratch,
        compiler_params=pltpu.CompilerParams(
            vmem_limit_bytes=58 << 20, collective_id=0, has_side_effects=True
        ),
        cost_estimate=pl.CostEstimate(
            flops=10_000_000_000, bytes_accessed=20_000_000, transcendentals=0
        ),
    )(
        in_place(doc_lengths), in_place(kda_query), in_place(kda_key), in_place(kda_value),
        in_place(log_decay), in_place(write_strength), in_place(mla_query), in_place(latents),
        in_place(value_up), in_place(out_proj),
    )
    if not exchange:
        mixed = lax.psum_scatter(mixed, "head", scatter_dimension=1, tiled=True)
        return kda_out, mixed
    return pl.pallas_call(
        write_out,
        in_specs=[pl.BlockSpec(memory_space=pltpu.VMEM)] * 2,
        out_specs=[anywhere] * 2,
        out_shape=[pltpu.HBM(kda_out.shape, bf16), pltpu.HBM(mixed.shape, bf16)],
        scratch_shapes=[dma((2,))],
        compiler_params=pltpu.CompilerParams(vmem_limit_bytes=4 << 20),
    )(
        pltpu.with_memory_space_constraint(kda_out, pltpu.VMEM),
        pltpu.with_memory_space_constraint(mixed, pltpu.VMEM),
    )


def solution(mesh):
    placed = (
        P(("group", "req"), "ctx", "head"),
        P(("group", "req"), "ctx", "head"),
        P(("group", "req"), "ctx", "head"),
        P(("group", "req"), "ctx", "head"),
        P(("group", "req"), "head", "ctx"),
        P(("group", "req"), "ctx", "head"),
        P(("group", "req"), "ctx", None),
        P("head", None, None),
        P("head", None),
        P(("group", "req"), None),
    )
    return jax.shard_map(
        local,
        mesh=mesh,
        in_specs=placed,
        out_specs=(P(("group", "req"), "ctx", "head"), P(("group", "req"), ("ctx", "head"), None)),
        check_vma=False,
    )
```
